512 devices in a mesh: expert: 32 (over z, core), tensor: 16 (over y, x).
Axes of the slice: x: 4, y: 4, z: 16, core: 2. Of those that a mesh axis runs over, the one named last changes fastest.
Arguments:
- hidden_in: bfloat16 [4096, 4096], P('expert', 'tensor'), may hold values from -92 to 92
- norm_gain: float32 [4096], P('tensor'), may hold values from 0.5 to 1.5
- expert_ids: int32 [4096, 8], P('expert'), may hold values from 0 to 63, all different within a row; in each aligned block of 128 rows (0 to 127, 128 to 255, ...) at most 24 rows name the same one
- route_weights: float32 [4096, 8], P('expert'), may hold values from 0.05 to 0.5
- w_gate: bfloat16 [64, 1536, 4096], P('expert', 'tensor'), may hold values from -0.09375 to 0.09375
- w_up: bfloat16 [64, 1536, 4096], P('expert', 'tensor'), may hold values from -0.09375 to 0.09375
- w_down: bfloat16 [64, 1536, 4096], P('expert', 'tensor'), may hold values from -0.15625 to 0.15625
Outputs:
- moe_out: bfloat16 [4096, 4096], P('expert', 'tensor')
The draws below stay inside these ranges and needn't reach their ends.
Inputs may be any that keep to these rules, and one draw needn't show every extreme that they name: `expert_ids`: in each aligned block of 128 rows (the rows of one index of the expert axis) no expert is named by more than 24 rows, a bound that some block reaches.
All inputs are finite; a program needn't handle non-finite values.
Results may differ from the reference program's by a relative error of at most 0.019.
Values may be sent and summed in bfloat16 or wider, within the bound.
A program may use at most 128 MiB of HBM per device.

```python
import math
import jax
import jax.numpy as jnp
import numpy as np
from jax import lax

D = 4096
FF = 1536
TOPK = 8
TOK_DEV = 128
EXPERTS = 64
TOKENS = 4096
CAP = 24
N_EXPERT = 32
N_TENSOR = 16


def draw_hidden_in(key, part):
    first, second = jax.random.split(key, 2)
    column = jnp.arange(D, dtype=jnp.float32) / D
    level = jax.random.uniform(second, (TOKENS, 1), jnp.float32, 0.0, 1.0)
    base = jnp.clip(jax.random.normal(first, (TOKENS, D), jnp.float32), -4.0, 4.0)
    scale = 10.0 ** level * (3.0 ** column)[None, :] * 0.5
    return (base * scale).astype(jnp.bfloat16)


def steps_of(stream_key, dims, shards, smallest, largest):
    def one(dim, blocks):
        draws = jax.random.uniform(jax.random.fold_in(jax.random.fold_in(stream_key, 6), dim), (blocks,), jnp.float32, smallest / len(shards), largest / len(shards))
        return jnp.repeat(jnp.exp(draws), dims[dim] // blocks).reshape((-1,) + (1,) * (len(dims) - dim - 1))

    factor_of = one(*shards[0])
    for cut in shards[1:]:
        factor_of = factor_of * one(*cut)
    return factor_of


def assign_block(rng, own, number, rows, amount, top, most, lean):
    sequence = jax.random.permutation(rng, amount)
    crowded, usual = portions_of(amount, rows * top, most, lean, True), portions_of(amount, rows * top, most, lean, False)
    places = jnp.arange(amount)

    def named(tallies, offset_by):
        used = int((tallies > 0).sum())
        fixed = max(1, used // 4)
        shifted = fixed + (places - fixed + offset_by * (used - fixed)) % max(1, amount - fixed)
        return jnp.zeros((amount,), jnp.int32).at[sequence[jnp.where(places < fixed, places, shifted)]].set(jnp.asarray(tallies, jnp.int32))

    tallies = jnp.where(number % 4 == 0, named(crowded, number // 4), named(usual, number - number // 4 - 1))
    mixed = jax.random.permutation(jax.random.fold_in(own, 3), amount)
    source_of, taker = mixed[0:amount // 2 * 2:2], mixed[1:amount // 2 * 2:2]
    slack = jnp.minimum(tallies[source_of] - 1, most - tallies[taker]) // 2
    slack = jnp.where((source_of == sequence[0]) | (taker == sequence[0]) | (tallies[taker] == 0), 0, jnp.maximum(slack, 0))
    shifted = jax.random.randint(jax.random.fold_in(own, 4), (amount // 2,), 0, 1 << 20) % (slack + 1)
    tallies = tallies.at[source_of].add(-shifted).at[taker].add(shifted)
    items = jnp.searchsorted(jnp.cumsum(tallies), jnp.arange(rows * top), side="right").astype(jnp.int32)
    table = items.reshape(top, rows).T
    table = table[jax.random.permutation(jax.random.fold_in(own, 1), rows)]
    offset_by = jax.random.randint(jax.random.fold_in(own, 2), (rows, 1), 0, top)
    return jnp.take_along_axis(table, (jnp.arange(top)[None, :] + offset_by) % top, axis=1)


def portions_of(amount, total, reach, lean, full):
    loads = [(1 << 20) // math.isqrt(standing ** lean) + 1 for standing in range(1, amount + 1)]
    largest = reach if full else min(reach, max(-(-total // amount), total * loads[0] // sum(loads)))
    least = 1 if total - largest >= amount - 1 else 0
    given, rest = [largest] + [least] * (amount - 1), total - largest - least * (amount - 1)
    while rest > 0:
        movable = [i for i in range(1, amount) if given[i] < largest] or [i for i in range(1, amount) if given[i] < reach]
        whole, remaining = sum([loads[i] for i in movable]), rest
        for i in movable:
            addition = min(reach - given[i], max(1, remaining * loads[i] // whole), rest)
            given[i] = given[i] + addition
            rest = rest - addition
    return np.array(given)


def centred(stream_key, dims, width, bound, shards=(), held_as=jnp.bfloat16):
    values = width * jax.random.normal(stream_key, dims, jnp.float32)
    if shards:
        values = values * steps_of(stream_key, dims, shards, -0.22, 0.18)
    return jnp.clip(values, -bound, bound).astype(held_as)


def setup_inputs(seed: int = 0) -> dict:
    key_list = jax.random.split(jax.random.key(seed), 8)
    hidden_in = draw_hidden_in(jax.random.fold_in(key_list[7], 71), 0)
    norm_gain = jnp.clip(1.0 + 0.1 * jax.random.normal(key_list[1], (D,), jnp.float32), 0.5, 1.5)
    expert_ids_keys = jax.random.split(jax.random.fold_in(key_list[2], 1), TOKENS // TOK_DEV)
    expert_ids_turns = jax.random.permutation(jax.random.fold_in(key_list[2], 3), TOKENS // TOK_DEV)
    expert_ids = jax.vmap(lambda own, number: assign_block(jax.random.fold_in(key_list[2], 2), own, number, TOK_DEV, EXPERTS, TOPK, CAP, 2))(expert_ids_keys, expert_ids_turns).reshape((TOKENS, TOPK))
    route_weights = jnp.clip(jnp.exp(math.log(0.5) - 2.3025851 * jax.random.uniform(key_list[3], (TOKENS, TOPK), jnp.float32) ** steps_of(key_list[3], (TOKENS, TOPK), ((0, 32),), -0.2, 0.2)), 0.05, 0.5)
    w_gate = centred(key_list[4], (EXPERTS, FF, D), D ** -0.5, 0.09375, ((0, 32), (1, 16)))
    w_up = centred(key_list[5], (EXPERTS, FF, D), D ** -0.5, 0.09375, ((0, 32), (1, 16)))
    w_down = centred(key_list[6], (EXPERTS, FF, D), FF ** -0.5, 0.15625, ((0, 32), (1, 16)))
    return dict(hidden_in=hidden_in, norm_gain=norm_gain, expert_ids=expert_ids, route_weights=route_weights, w_gate=w_gate, w_up=w_up, w_down=w_down)


epsilon = 1e-06

def reference(hidden_in, norm_gain, expert_ids, route_weights, w_gate, w_up, w_down):
    widened = hidden_in.astype(jnp.float32)
    squares = lax.optimization_barrier(jnp.sum(widened * widened, axis=1, keepdims=True))
    normed = (widened * lax.rsqrt(squares / D + epsilon) * norm_gain[None, :]).astype(jnp.bfloat16)
    blocks = expert_ids.reshape(N_EXPERT, TOK_DEV, TOPK)
    picked_mask = (blocks[:, :, :, None] == jnp.arange(EXPERTS, dtype=jnp.int32)[None, None, None, :]).astype(jnp.int32)
    chosen = lax.optimization_barrier(jnp.sum(picked_mask, axis=2))
    before = jnp.cumsum(chosen, axis=1) - chosen
    position = lax.optimization_barrier(jnp.sum(picked_mask * before[:, :, None, :], axis=3))
    source = jnp.arange(N_EXPERT, dtype=jnp.int32)[:, None, None]
    row_index = ((blocks * N_EXPERT + source) * CAP + position).reshape(TOKENS * TOPK).astype(jnp.int32)
    spread_rows = jnp.repeat(normed, TOPK, axis=0)
    dense = jnp.zeros((EXPERTS * N_EXPERT * CAP, D), jnp.bfloat16).at[row_index].set(spread_rows)
    dense = dense.reshape(EXPERTS, N_EXPERT * CAP, D)
    group = FF // N_TENSOR
    contract = (((1,), (1,)), ((), ()))

    def one_expert(operands):
        rows, gate_w, up_w, down_w = operands
        gate = lax.dot_general(rows, gate_w, contract, preferred_element_type=jnp.float32)
        up_val = lax.dot_general(rows, up_w, contract, preferred_element_type=jnp.float32)
        inner = (jax.nn.silu(gate) * up_val).astype(jnp.bfloat16)
        split_inner = inner.reshape(rows.shape[0], N_TENSOR, group).astype(jnp.float32)
        split_down = down_w.reshape(N_TENSOR, group, D).astype(jnp.float32)
        parts = jnp.einsum('rgf,gfd->grd', split_inner, split_down)
        rounded = lax.optimization_barrier(parts.astype(jnp.bfloat16))
        return lax.optimization_barrier(jnp.sum(rounded.astype(jnp.float32), axis=0))
    outputs = lax.map(one_expert, (dense, w_gate, w_up, w_down))
    lookup = outputs.reshape(EXPERTS * N_EXPERT * CAP, D)
    gathered = lookup[row_index].reshape(TOKENS, TOPK, D)
    mixed = lax.optimization_barrier(jnp.sum(gathered * route_weights[:, :, None], axis=1))
    return mixed.astype(jnp.bfloat16)
```

```python
import jax
import jax.numpy as jnp
from jax import lax
from jax.sharding import PartitionSpec as P

D = 4096


epsilon = 1e-06


def body(hidden_in, norm_gain, expert_ids, route_weights, w_gate, w_up, w_down):
    tokens_here = hidden_in.shape[0]
    choices_count = expert_ids.shape[1]
    exp_local = w_gate.shape[0]
    groups = lax.axis_size("expert")
    experts_all = exp_local * groups
    capacity = min(tokens_here, 3 * tokens_here * choices_count // (2 * experts_all))
    widened = hidden_in.astype(jnp.float32)
    squares = lax.psum(jnp.sum(widened * widened, axis=1), "tensor")
    normed = (widened * lax.rsqrt(squares / D + epsilon)[:, None] * norm_gain[None, :]).astype(
        jnp.bfloat16
    )
    routing = jnp.concatenate([expert_ids.astype(jnp.float32), route_weights], axis=1)
    routing = lax.all_gather(routing.T, "expert", axis=0, tiled=False)
    tokens_all = lax.all_gather(normed, "expert", axis=0, tiled=False)
    first = (lax.axis_index("expert") * exp_local).astype(jnp.float32)
    named = routing[:, None, :choices_count, :] == (
        first + jnp.arange(exp_local, dtype=jnp.float32)[None, :, None, None]
    )
    chosen = jnp.any(named, axis=2)
    scale = jnp.sum(jnp.where(named, routing[:, None, choices_count:, :], 0.0), axis=2)
    step = jnp.arange(tokens_here, dtype=jnp.int32)
    earlier = (step[:, None] < step[None, :]).astype(jnp.bfloat16)
    position = jnp.einsum(
        "bjs,st->bjt", chosen.astype(jnp.bfloat16), earlier, preferred_element_type=jnp.float32
    )
    slot = jnp.arange(capacity, dtype=jnp.float32)
    select = (
        (position[:, :, None, :] == slot[None, None, :, None]) & chosen[:, :, None, :]
    ).astype(jnp.bfloat16)
    rows = jnp.einsum(
        "bjst,btd->bjsd", select, tokens_all, preferred_element_type=jnp.float32
    ).astype(jnp.bfloat16)
    rows = rows.transpose(1, 0, 2, 3).reshape(exp_local, groups * capacity, -1)
    piece = lax.all_gather(rows, "tensor", axis=2, tiled=True)
    gate_add = jnp.einsum("erd,efd->erf", piece, w_gate, preferred_element_type=jnp.float32)
    up_add = jnp.einsum("erd,efd->erf", piece, w_up, preferred_element_type=jnp.float32)
    inner = (jax.nn.silu(gate_add) * up_add).astype(jnp.bfloat16)
    partials = jnp.einsum(
        "erf,efd->erd", inner, w_down, preferred_element_type=jnp.float32
    ).astype(jnp.bfloat16)
    summed = lax.psum_scatter(partials, "tensor", scatter_dimension=2, tiled=True)
    summed = summed.reshape(exp_local, groups, capacity, -1)
    back = jnp.einsum(
        "bjst,jbsd->bjtd", select, summed, preferred_element_type=jnp.float32
    )
    weighted = jnp.sum(back * scale[:, :, :, None], axis=1).astype(jnp.bfloat16)
    return lax.psum_scatter(weighted, "expert", scatter_dimension=0, tiled=False)


def solution(mesh):
    placed = (
        P("expert", "tensor"),
        P("tensor"),
        P("expert", None),
        P("expert", None),
        P("expert", "tensor", None),
        P("expert", "tensor", None),
        P("expert", "tensor", None),
    )
    return jax.shard_map(
        body, mesh=mesh, in_specs=placed, out_specs=P("expert", "tensor"), check_vma=False
    )
```

```python
import functools

import jax
import jax.numpy as jnp
from jax import lax
from jax.experimental import pallas as pl
from jax.experimental.pallas import tpu as pltpu
from jax.sharding import PartitionSpec as P

epsilon = 1e-06
SIDE = 4
BF = jnp.bfloat16
F32 = jnp.float32


def dot(a, b, ca, cb):
    return lax.dot_general(a, b, (((ca,), (cb,)), ((), ())), preferred_element_type=F32)


def kernel(
    Z, capacity, width,
    hid, gain, route, w_gate, w_up, w_down, out,
    tok, rows, gath, wts, accg, accu, inner, part, hop, from_l, from_r, vsum, cross, final,
    sw, cont, sib, zin, sqb,
    sq_s, sq_r, za_s, za_r, sb_s, sb_r, wl_r, w_s, w_r, a_s, a_r, b_s, b_r, f_s, f_r,
    r1_s, r1_r, r2_s, r2_r, c_s, c_r, cs_s, cs_r, q_s, q_r,
):
    H = Z // 2
    A = H // 2
    n = hid.shape[0]
    wide = hid.shape[1]
    fh = w_gate.shape[1]
    topk = route.shape[0] // 2
    experts = 4 * Z
    two = 2 * capacity
    half_rows = H * two

    E = lax.axis_index("expert")
    T = lax.axis_index("tensor")
    z, c = lax.div(E, 2), lax.rem(E, 2)
    y, x = lax.div(T, SIDE), lax.rem(T, SIDE)

    def mod(v, m):
        return lax.rem(v + m, m)

    def axes(j):
        return (x + j * (y - x), y + j * (x - y))

    def device(j, a, b):
        return (E, (b + j * (a - b)) * SIDE + a + j * (b - a))

    def column(j, sh):
        bb, aa = lax.div(sh, SIDE), lax.rem(sh, SIDE)
        t = bb * SIDE + aa + j * (aa * SIDE + bb - bb * SIDE - aa)
        return pl.ds(pl.multiple_of(t * wide, wide), wide)

    def send(src, dst, ssem, rsem, to):
        pltpu.make_async_remote_copy(
            src_ref=src, dst_ref=dst, send_sem=ssem, recv_sem=rsem,
            device_id=to, device_id_type=pl.DeviceIdType.MESH,
        ).start()

    def got(dst, ssem, rsem):
        pltpu.make_async_remote_copy(
            src_ref=dst, dst_ref=dst, send_sem=ssem, recv_sem=rsem,
            device_id=(E, T), device_id_type=pl.DeviceIdType.MESH,
        ).wait_recv()

    def left(src, ssem, rsem):
        pltpu.make_async_remote_copy(
            src_ref=src, dst_ref=src, send_sem=ssem, recv_sem=rsem,
            device_id=(E, T), device_id_type=pl.DeviceIdType.MESH,
        ).wait_send()

    other = (2 * z + 1 - c, T)
    z_up = (2 * mod(z + 1, Z) + c, T)
    z_down = (2 * mod(z - 1, Z) + c, T)

    barrier = pltpu.get_barrier_semaphore()
    partners = [other, z_up, z_down]
    for m in range(1, SIDE):
        partners.append((E, y * SIDE + mod(x + m, SIDE)))
        partners.append((E, mod(y + m, SIDE) * SIDE + x))
    for partner in partners:
        pl.semaphore_signal(barrier, inc=1, device_id=partner, device_id_type=pl.DeviceIdType.MESH)
    pl.semaphore_wait(barrier, len(partners))

    xx = hid[...].astype(F32)
    sq = jnp.sum(xx * xx, axis=1, keepdims=True)
    sqb[0, 0] = jnp.broadcast_to(sq, (n, 128)).T[0:8, :]
    for ph in range(2):
        for m in range(1, SIDE):
            to = (
                (E, y * SIDE + mod(x - m, SIDE)) if ph == 0 else (E, mod(y - m, SIDE) * SIDE + x)
            )
            send(sqb.at[ph, 0], sqb.at[ph, m], sq_s.at[ph, m], sq_r.at[ph, m], to)
        if ph == 0:
            ids = route[0:topk, :]
            wts_t = route[topk : 2 * topk, :]
            e_iota = lax.broadcasted_iota(jnp.int32, (experts, n), 0).astype(F32)
            hits = [e_iota == ids[k : k + 1, :] for k in range(topk)]
            chosen = jnp.zeros((experts, n), F32)
            for k in range(topk):
                chosen = chosen + jnp.where(hits[k], 1.0, 0.0)
            tri = (
                lax.broadcasted_iota(jnp.int32, (n, n), 0)
                < lax.broadcasted_iota(jnp.int32, (n, n), 1)
            ).astype(F32).astype(BF)
            before = dot(chosen.astype(BF), tri, 1, 0)
            pos = jnp.concatenate(
                [
                    jnp.sum(jnp.where(hits[k], before, 0.0), axis=0, keepdims=True)
                    for k in range(topk)
                ],
                axis=0,
            )
            high = wts_t.astype(BF).astype(F32)
            low = wts_t - high
            meta = jnp.concatenate(
                [jnp.concatenate([ids, high], axis=1), jnp.concatenate([low, pos], axis=1)], axis=0
            )
            tok[E, n : n + 2 * topk, :] = meta.astype(BF)
        for m in range(1, SIDE):
            got(sqb.at[ph, m], sq_s.at[ph, m], sq_r.at[ph, m])
        total = sqb[ph, 0] + sqb[ph, 1] + sqb[ph, 2] + sqb[ph, 3]
        if ph == 0:
            sqb[1, 0] = total
    scale = lax.rsqrt(total / width + epsilon)
    scale = jnp.broadcast_to(scale[0:1, :], (128, n)).T[:, 0:1]
    tok[E, 0:n, :] = (xx * scale * gain[...]).astype(BF)

    send(tok.at[E], tok.at[E], za_s.at[0, 0], za_r.at[0, 0], z_up)
    send(tok.at[E], tok.at[E], za_s.at[1, 0], za_r.at[1, 0], z_down)
    send(tok.at[E], tok.at[E], sb_s.at[0], sb_r.at[0], other)

    for j in range(2):
        a, b = axes(j)
        up = lax.rem(a + c, 2)
        mate = mod(a + 1 - 2 * up, SIDE)
        for i, w in enumerate((w_gate, w_up, w_down)):
            pltpu.make_async_copy(w.at[j], wts.at[j, i, pl.ds(0, fh)], wl_r.at[j, i]).start()
            send(w.at[j], wts.at[j, i, pl.ds(fh, fh)], w_s.at[j, i], w_r.at[j, i], device(j, mate, b))

    r_iota = lax.broadcasted_iota(jnp.int32, (two, 2 * n), 0).astype(F32)
    lane = lax.broadcasted_iota(jnp.int32, (1, 2 * n), 1)
    shift = jnp.where(lane >= n, float(capacity), 0.0)
    mine = (2 * E).astype(F32)

    def select(p, order):
        got(tok.at[2 * p + 1 - c], sb_s.at[order], sb_r.at[order])
        m0 = tok[2 * p, n : n + 2 * topk, :].astype(F32)
        m1 = tok[2 * p + 1, n : n + 2 * topk, :].astype(F32)

        def both(r, l):
            return jnp.concatenate(
                [
                    m0[r * topk : (r + 1) * topk, l * n : (l + 1) * n],
                    m1[r * topk : (r + 1) * topk, l * n : (l + 1) * n],
                ],
                axis=1,
            )

        ids, high, low, pos = both(0, 0), both(0, 1), both(1, 0), both(1, 1)
        picked = []
        for j in range(2):
            hit = ids == mine + float(j)
            named = jnp.sum(jnp.where(hit, 1.0, 0.0), axis=0, keepdims=True)
            slot = jnp.sum(jnp.where(hit, pos, 0.0), axis=0, keepdims=True)
            wh = jnp.sum(jnp.where(hit, high, 0.0), axis=0, keepdims=True)
            wo = jnp.sum(jnp.where(hit, low, 0.0), axis=0, keepdims=True)
            slot = jnp.where(named > 0.5, slot + shift, -1.0)
            chosen = jnp.where(r_iota == slot, 1.0, 0.0)
            sw[p, j * two : (j + 1) * two, :] = (chosen * wh).astype(BF)
            sw[p, (2 + j) * two : (3 + j) * two, :] = (chosen * wo).astype(BF)
            picked.append(chosen.astype(BF))
        pair = tok[pl.ds(2 * p, 2), 0:n, :].reshape(2 * n, wide)
        taken = dot(jnp.concatenate(picked, axis=0), pair, 1, 0).astype(BF)
        rows[0, p] = taken[0:two, :]
        rows[1, p] = taken[two : 2 * two, :]

    def z_step(s, carry):
        pr, po = mod(z - 1 - s, Z), mod(z + 1 + s, Z)
        br, bo = tok.at[2 * pr + c], tok.at[2 * po + c]
        got(br, za_s.at[0, s], za_r.at[0, s])

        @pl.when(s < H - 1)
        def _():
            send(br, br, za_s.at[0, s + 1], za_r.at[0, s + 1], z_up)

        send(br, br, sb_s.at[1 + s], sb_r.at[1 + s], other)

        @pl.when(s < H - 1)
        def _():
            got(bo, za_s.at[1, s], za_r.at[1, s])

            @pl.when(s < H - 2)
            def _():
                send(bo, bo, za_s.at[1, s + 1], za_r.at[1, s + 1], z_down)

            send(bo, bo, sb_s.at[1 + H + s], sb_r.at[1 + H + s], other)

        select(mod(z - s, Z), s)

        @pl.when(s > 0)
        def _():
            select(mod(z + s, Z), H + s)

        return carry

    lax.fori_loop(0, H, z_step, 0)
    select(mod(z - H, Z), H)

    for j in range(2):
        a, b = axes(j)
        sh = b * SIDE + a
        pltpu.make_async_copy(
            rows.at[j, pl.ds(H * lax.rem(a, 2), H)], gath.at[j, sh], a_r.at[j, 0]
        ).start()
        for k in (1, 3, 2):
            to = mod(a - k, SIDE)
            send(
                rows.at[j, pl.ds(H * lax.rem(to, 2), H)], gath.at[j, sh],
                a_s.at[j, k], a_r.at[j, k], device(j, to, b),
            )
    accg[...] = jnp.zeros_like(accg)
    accu[...] = jnp.zeros_like(accu)
    for j in range(2):
        a, b = axes(j)
        pltpu.make_async_copy(
            rows.at[j, pl.ds(H * lax.rem(a, 2), H)], gath.at[j, b * SIDE + a], a_r.at[j, 0]
        ).wait()
        for i, w in enumerate((w_gate, w_up, w_down)):
            pltpu.make_async_copy(w.at[j], wts.at[j, i, pl.ds(0, fh)], wl_r.at[j, i]).wait()

    def forward_own(j, k):
        a, b = axes(j)
        sh = b * SIDE + mod(a + k, SIDE)
        piece = gath.at[j, sh]
        send(piece, piece, b_s.at[j, k, 0], b_r.at[j, k, 0], device(j, a, mod(b + 1, SIDE)))
        send(piece, piece, b_s.at[j, k, 1], b_r.at[j, k, 1], device(j, a, mod(b - 1, SIDE)))

    for j in range(2):
        forward_own(j, 0)
    for j in range(2):
        for i in range(3):
            got(wts.at[j, i, pl.ds(fh, fh)], w_s.at[j, i], w_r.at[j, i])

    def multiply(j, sh):
        piece = gath[j, sh].reshape(half_rows, wide)
        col = column(j, sh)
        accg[j] += dot(piece, wts[j, 0, :, col], 1, 1)
        accu[j] += dot(piece, wts[j, 1, :, col], 1, 1)

    def gather_near(i, carry):
        j, k = lax.rem(i, 2), lax.div(i, 2)
        a, b = axes(j)
        sh = b * SIDE + mod(a + k, SIDE)

        @pl.when(k > 0)
        def _():
            got(gath.at[j, sh], a_s.at[j, k], a_r.at[j, k])
            forward_own(j, k)

        multiply(j, sh)
        return carry

    lax.fori_loop(0, 2 * SIDE, gather_near, 0)

    def gather_side(i, carry):
        j, k = lax.rem(i, 2), lax.div(i, 2)
        a, b = axes(j)
        low = mod(b - 1, SIDE) * SIDE + mod(a + k, SIDE)
        high = mod(b + 1, SIDE) * SIDE + mod(a + k, SIDE)
        got(gath.at[j, low], b_s.at[j, k, 0], b_r.at[j, k, 0])

        @pl.when(lax.rem(k, 2) == 0)
        def _():
            piece = gath.at[j, low]
            send(piece, piece, f_s.at[j, k], f_r.at[j, k], device(j, a, mod(b + 1, SIDE)))

        got(gath.at[j, high], b_s.at[j, k, 1], b_r.at[j, k, 1])

        @pl.when(lax.rem(k, 2) == 1)
        def _():
            piece = gath.at[j, high]
            send(piece, piece, f_s.at[j, k], f_r.at[j, k], device(j, a, mod(b - 1, SIDE)))

        multiply(j, low)
        multiply(j, high)
        return carry

    lax.fori_loop(0, 2 * SIDE, gather_side, 0)

    def gather_far(i, carry):
        j, k = lax.rem(i, 2), lax.div(i, 2)
        a, b = axes(j)
        sh = mod(b + 2, SIDE) * SIDE + mod(a + k, SIDE)
        got(gath.at[j, sh], f_s.at[j, k], f_r.at[j, k])
        multiply(j, sh)
        return carry

    lax.fori_loop(0, 2 * SIDE, gather_far, 0)

    for j in range(2):
        g = accg[j]
        inner[j] = (g / (1.0 + jnp.exp(-g)) * accu[j]).astype(BF)

    for d in (2, 1, 3, 0):
        for j in range(2):
            a, b = axes(j)
            first = mod(b + d, SIDE) * SIDE

            def down(aa, carry, j=j, first=first):
                sh = first + aa
                made = dot(inner[j], wts[j, 2, :, column(j, sh)], 1, 0).astype(BF)
                part[j, sh] = made.reshape(H, two, wide)
                return carry

            lax.fori_loop(0, SIDE, down, 0)
            bundle = part.at[j, pl.ds(first, SIDE)]
            above, below = device(j, a, mod(b + 1, SIDE)), device(j, a, mod(b - 1, SIDE))
            lo, hi = pl.ds(0, A), pl.ds(A, A)
            if d == 2:
                send(bundle.at[:, lo], hop.at[j, 0], r1_s.at[j, 0], r1_r.at[j, 0], above)
                send(bundle.at[:, hi], hop.at[j, 1], r1_s.at[j, 1], r1_r.at[j, 1], below)
            elif d == 1:
                send(bundle.at[:, hi], from_l.at[j, :, hi], r1_s.at[j, 2], r1_r.at[j, 2], above)
            elif d == 3:
                send(bundle.at[:, lo], from_r.at[j, :, lo], r1_s.at[j, 3], r1_r.at[j, 3], below)

    lo, hi = pl.ds(0, A), pl.ds(A, A)
    for j in range(2):
        a, b = axes(j)
        above, below = device(j, a, mod(b + 1, SIDE)), device(j, a, mod(b - 1, SIDE))
        for side, (d, cut, target, to) in enumerate(
            ((1, lo, from_l, above), (3, hi, from_r, below))
        ):
            first = mod(b + d, SIDE) * SIDE
            got(hop.at[j, side], r1_s.at[j, side], r1_r.at[j, side])

            def add_hop(aa, carry, j=j, first=first, cut=cut, side=side):
                mixed = part[j, first + aa, cut].astype(F32) + hop[j, side, aa].astype(F32)
                part[j, first + aa, cut] = mixed.astype(BF)
                return carry

            lax.fori_loop(0, SIDE, add_hop, 0)
            send(
                part.at[j, pl.ds(first, SIDE), cut], target.at[j, :, cut],
                r2_s.at[j, side], r2_r.at[j, side], to,
            )

    for j in range(2):
        a, b = axes(j)
        got(from_l.at[j, :, hi], r1_s.at[j, 2], r1_r.at[j, 2])
        got(from_r.at[j, :, lo], r1_s.at[j, 3], r1_r.at[j, 3])
        got(from_l.at[j, :, lo], r2_s.at[j, 0], r2_r.at[j, 0])
        got(from_r.at[j, :, hi], r2_s.at[j, 1], r2_r.at[j, 1])
        for m in (2, 1, 3, 0):
            aa = mod(a + m, SIDE)
            mixed = (
                part[j, b * SIDE + aa].astype(F32)
                + from_l[j, aa].astype(F32)
                + from_r[j, aa].astype(F32)
            )
            vsum[j, m] = mixed.astype(BF)
            if m:
                send(vsum.at[j, m], cross.at[j, m], c_s.at[j, m], c_r.at[j, m], device(j, aa, b))
    for j in range(2):
        a, b = axes(j)
        own = lax.rem(a, 2)
        for m in (1, 3, 2):
            got(cross.at[j, m], c_s.at[j, m], c_r.at[j, m])
        final[j, pl.ds(H * (1 - own), H)] = (
            cross[j, 1].astype(F32) + cross[j, 3].astype(F32)
        ).astype(BF)
        final[j, pl.ds(H * own, H)] = (vsum[j, 0].astype(F32) + cross[j, 2].astype(F32)).astype(BF)

    def combine(p):
        stacked = jnp.concatenate([final[0, p], final[1, p]], axis=0)
        stacked = jnp.concatenate([stacked, stacked], axis=0)
        made = dot(sw[p], stacked, 0, 0).astype(BF)
        cont[p, 0] = made[0:n, :]
        cont[p, 1] = made[n : 2 * n, :]
        send(cont.at[p, 1 - c], sib.at[p], cs_s.at[p], cs_r.at[p], other)

    hn = n // 2

    def spots(s):
        return mod(z + H - s, Z), mod(z + H + 1 + s, Z)

    for p in spots(0):
        combine(p)

    def ring(s, carry):
        p1, p2 = spots(s)

        @pl.when(s < H - 1)
        def _():
            for p in spots(s + 1):
                combine(p)

        for way, p, to in ((0, p1, z_up), (1, p2, z_down)):
            got(sib.at[p], cs_s.at[p], cs_r.at[p])

            for u in range(2):
                cut = pl.ds(u * hn, hn)

                @pl.when(s == 0)
                def _():
                    cont[p, c, cut] = (
                        cont[p, c, cut].astype(F32) + sib[p, cut].astype(F32)
                    ).astype(BF)

                @pl.when(s > 0)
                def _():
                    got(zin.at[way, s - 1, cut], q_s.at[way, s - 1, u], q_r.at[way, s - 1, u])
                    cont[p, c, cut] = (
                        cont[p, c, cut].astype(F32)
                        + sib[p, cut].astype(F32)
                        + zin[way, s - 1, cut].astype(F32)
                    ).astype(BF)

                @pl.when(s + way < H)
                def _():
                    send(
                        cont.at[p, c, cut], zin.at[way, s, cut],
                        q_s.at[way, s, u], q_r.at[way, s, u], to,
                    )

        return carry

    lax.fori_loop(0, H, ring, 0)
    for u in range(2):
        cut = pl.ds(u * hn, hn)
        got(zin.at[0, H - 1, cut], q_s.at[0, H - 1, u], q_r.at[0, H - 1, u])
        out[cut] = (cont[z, c, cut].astype(F32) + zin[0, H - 1, cut].astype(F32)).astype(BF)

    for ph in range(2):
        for m in range(1, SIDE):
            left(sqb.at[ph, 0], sq_s.at[ph, m], sq_r.at[ph, m])

    def left_z(s, carry):
        left(tok.at[0], za_s.at[0, s], za_r.at[0, s])

        @pl.when(s < H - 1)
        def _():
            left(tok.at[0], za_s.at[1, s], za_r.at[1, s])

        for u in range(2):
            cut = pl.ds(u * hn, hn)
            left(zin.at[0, 0, cut], q_s.at[0, s, u], q_r.at[0, s, u])

            @pl.when(s < H - 1)
            def _():
                left(zin.at[1, 0, cut], q_s.at[1, s, u], q_r.at[1, s, u])

        return carry

    lax.fori_loop(0, H, left_z, 0)

    def left_pairs(p, carry):
        left(tok.at[0], sb_s.at[p], sb_r.at[p])
        left(sib.at[0], cs_s.at[p], cs_r.at[p])
        return carry

    lax.fori_loop(0, Z, left_pairs, 0)
    for j in range(2):
        for i, w in enumerate((w_gate, w_up, w_down)):
            left(w.at[j], w_s.at[j, i], w_r.at[j, i])
        for k in range(1, SIDE):
            left(rows.at[j, pl.ds(0, H)], a_s.at[j, k], a_r.at[j, k])
            left(vsum.at[j, k], c_s.at[j, k], c_r.at[j, k])
        for k in range(SIDE):
            left(gath.at[j, 0], b_s.at[j, k, 0], b_r.at[j, k, 0])
            left(gath.at[j, 0], b_s.at[j, k, 1], b_r.at[j, k, 1])
            left(gath.at[j, 0], f_s.at[j, k], f_r.at[j, k])
            left(hop.at[j, 0], r1_s.at[j, k], r1_r.at[j, k])
        for k in range(2):
            left(hop.at[j, 0], r2_s.at[j, k], r2_r.at[j, k])


def body(hidden_in, norm_gain, expert_ids, route_weights, w_gate, w_up, w_down):
    n, wide = hidden_in.shape
    topk = expert_ids.shape[1]
    fh = w_gate.shape[1]
    groups = lax.axis_size("expert")
    Z = groups // 2
    H = Z // 2
    capacity = min(n, 3 * n * topk // (2 * 2 * groups))
    two = 2 * capacity
    route = jnp.concatenate([expert_ids.astype(F32), route_weights], axis=1).T
    vm, dma = pltpu.VMEM, pltpu.SemaphoreType.DMA
    shards = SIDE * SIDE
    scratch = [
        vm((groups, n + 2 * topk, wide), BF),
        vm((2, Z, two, wide), BF),
        vm((2, shards, H, two, wide), BF),
        vm((2, 3, 2 * fh, shards * wide), BF),
        vm((2, H * two, 2 * fh), F32),
        vm((2, H * two, 2 * fh), F32),
        vm((2, H * two, 2 * fh), BF),
        vm((2, shards, H, two, wide), BF),
        vm((2, 2, SIDE, H // 2, two, wide), BF),
        vm((2, SIDE, H, two, wide), BF),
        vm((2, SIDE, H, two, wide), BF),
        vm((2, SIDE, H, two, wide), BF),
        vm((2, SIDE, H, two, wide), BF),
        vm((2, Z, two, wide), BF),
        vm((Z, 4 * two, 2 * n), BF),
        vm((Z, 2, n, wide), BF),
        vm((Z, n, wide), BF),
        vm((2, H, n, wide), BF),
        vm((2, SIDE, 8, n), F32),
        dma((2, SIDE)), dma((2, SIDE)),
        dma((2, H)), dma((2, H)),
        dma((Z,)), dma((Z,)),
        dma((2, 3)), dma((2, 3)), dma((2, 3)),
        dma((2, SIDE)), dma((2, SIDE)),
        dma((2, SIDE, 2)), dma((2, SIDE, 2)),
        dma((2, SIDE)), dma((2, SIDE)),
        dma((2, SIDE)), dma((2, SIDE)),
        dma((2, 2)), dma((2, 2)),
        dma((2, SIDE)), dma((2, SIDE)),
        dma((Z,)), dma((Z,)),
        dma((2, H, 2)), dma((2, H, 2)),
    ]
    vmem = pl.BlockSpec(memory_space=pltpu.VMEM)
    anywhere = pl.BlockSpec(memory_space=pl.ANY)
    return pl.pallas_call(
        functools.partial(kernel, Z, capacity, wide * shards),
        out_shape=jax.ShapeDtypeStruct((n, wide), BF),
        in_specs=[vmem, vmem, vmem, anywhere, anywhere, anywhere],
        out_specs=vmem,
        scratch_shapes=scratch,
        compiler_params=pltpu.CompilerParams(
            collective_id=0, has_side_effects=True, vmem_limit_bytes=58 * 2**20
        ),
    )(hidden_in, norm_gain[None, :], route, w_gate, w_up, w_down)


def solution(mesh):
    placed = (
        P("expert", "tensor"),
        P("tensor"),
        P("expert", None),
        P("expert", None),
        P("expert", "tensor", None),
        P("expert", "tensor", None),
        P("expert", "tensor", None),
    )
    return jax.shard_map(
        body, mesh=mesh, in_specs=placed, out_specs=P("expert", "tensor"), check_vma=False
    )
```

```python
import functools

import jax
import jax.numpy as jnp
from jax import lax
from jax.experimental import pallas as pl
from jax.experimental.pallas import tpu as pltpu
from jax.sharding import PartitionSpec as P

epsilon = 1e-06
SIDE = 4
BF = jnp.bfloat16
F32 = jnp.float32


def dot(a, b, ca, cb):
    return lax.dot_general(a, b, (((ca,), (cb,)), ((), ())), preferred_element_type=F32)


def kernel(
    Z, capacity, width,
    hid, gain, ids_in, weights_in, w_gate, w_up, w_down, out,
    tok, rows, gath, wts, accg, accu, ssq, inner, part, hop, from_l, from_r, vsum, cross, final,
    sw, cont, sib, zin, gains,
    gn_s, gn_r, za_s, za_r, sb_s, sb_r, wl_r, w_s, w_r, a_s, a_r, b_s, b_r, f_s, f_r,
    r1_s, r1_r, r2_s, r2_r, c_s, c_r, cs_s, cs_r, q_s, q_r,
):
    H = Z // 2
    Q = H // 2
    A = Q // 2
    n, wide = hid.shape
    fh = w_gate.shape[1]
    topk = ids_in.shape[1]
    experts = 4 * Z
    two = 2 * capacity
    chunk_rows = Q * two
    mesh_ids = pl.DeviceIdType.MESH

    E = lax.axis_index("expert")
    T = lax.axis_index("tensor")
    z, c = lax.div(E, 2), lax.rem(E, 2)
    y, x = lax.div(T, SIDE), lax.rem(T, SIDE)

    def mod(v, m):
        return lax.rem(v + m, m)

    def axes(j):
        return (x + j * (y - x), y + j * (x - y))

    def device(j, a, b):
        return (E, (b + j * (a - b)) * SIDE + a + j * (b - a))

    def owner(j, sh):
        bb, aa = lax.div(sh, SIDE), lax.rem(sh, SIDE)
        return bb * SIDE + aa + j * (aa * SIDE + bb - bb * SIDE - aa)

    def column(j, sh):
        return pl.ds(pl.multiple_of(owner(j, sh) * wide, wide), wide)

    def send(src, dst, ssem, rsem, to):
        pltpu.make_async_remote_copy(
            src_ref=src, dst_ref=dst, send_sem=ssem, recv_sem=rsem,
            device_id=to, device_id_type=mesh_ids,
        ).start()

    def got(dst, ssem, rsem):
        pltpu.make_async_remote_copy(
            src_ref=dst, dst_ref=dst, send_sem=ssem, recv_sem=rsem,
            device_id=(E, T), device_id_type=mesh_ids,
        ).wait_recv()

    def left(src, ssem, rsem):
        pltpu.make_async_remote_copy(
            src_ref=src, dst_ref=src, send_sem=ssem, recv_sem=rsem,
            device_id=(E, T), device_id_type=mesh_ids,
        ).wait_send()

    other = (2 * z + 1 - c, T)
    z_up = (2 * mod(z + 1, Z) + c, T)
    z_down = (2 * mod(z - 1, Z) + c, T)

    barrier = pltpu.get_barrier_semaphore()
    partners = [other, z_up, z_down]
    for m in range(1, SIDE):
        partners.append((E, y * SIDE + mod(x + m, SIDE)))
        partners.append((E, mod(y + m, SIDE) * SIDE + x))
    for partner in partners:
        pl.semaphore_signal(barrier, inc=1, device_id=partner, device_id_type=mesh_ids)

    ids = ids_in[...].astype(F32).T
    wts_t = weights_in[...].T
    e_iota = lax.broadcasted_iota(jnp.int32, (experts, n), 0).astype(F32)
    hits = [e_iota == ids[k : k + 1, :] for k in range(topk)]
    chosen = jnp.zeros((experts, n), F32)
    for k in range(topk):
        chosen = chosen + jnp.where(hits[k], 1.0, 0.0)
    tri = (
        lax.broadcasted_iota(jnp.int32, (n, n), 0) < lax.broadcasted_iota(jnp.int32, (n, n), 1)
    ).astype(F32).astype(BF)
    before = dot(chosen.astype(BF), tri, 1, 0)
    pos = jnp.concatenate(
        [jnp.sum(jnp.where(hits[k], before, 0.0), axis=0, keepdims=True) for k in range(topk)],
        axis=0,
    )
    high = wts_t.astype(BF).astype(F32)
    meta = jnp.concatenate(
        [jnp.concatenate([ids, high], axis=1), jnp.concatenate([wts_t - high, pos], axis=1)],
        axis=0,
    )
    tok[E, n : n + 2 * topk, :] = meta.astype(BF)
    tok[E, 0:n, :] = hid[...]
    gains[T] = jnp.broadcast_to(gain[...], (8, wide))
    for j in range(2):
        for i, w in enumerate((w_gate, w_up, w_down)):
            pltpu.make_async_copy(w.at[j], wts.at[j, i, pl.ds(0, fh)], wl_r.at[j, i]).start()
    pl.semaphore_wait(barrier, len(partners))

    nb = 16 * ((n + 2 * topk + 31) // 32)
    cuts = [pl.ds(0, nb), pl.ds(nb, n + 2 * topk - nb)]
    for u in range(2):
        mine = tok.at[E, cuts[u]]
        send(mine, mine, za_s.at[0, 0, u], za_r.at[0, 0, u], z_up)
        send(mine, mine, za_s.at[1, 0, u], za_r.at[1, 0, u], z_down)
    send(tok.at[E], tok.at[E], sb_s.at[0], sb_r.at[0], other)
    for m in range(1, SIDE):
        to = (E, y * SIDE + mod(x + m, SIDE))
        send(gains.at[T], gains.at[T], gn_s.at[0, m], gn_r.at[0, m], to)

    for j in range(2):
        a, b = axes(j)
        mate = mod(a + 1 - 2 * lax.rem(a + c, 2), SIDE)
        for i, w in enumerate((w_gate, w_up, w_down)):
            send(w.at[j], wts.at[j, i, pl.ds(fh, fh)], w_s.at[j, i], w_r.at[j, i], device(j, mate, b))

    for m in range(1, SIDE):
        got(gains.at[y * SIDE + mod(x - m, SIDE)], gn_s.at[0, m], gn_r.at[0, m])
    line = gains.at[pl.ds(y * SIDE, SIDE)]
    for m in range(1, SIDE):
        to = (E, mod(y + m, SIDE) * SIDE + x)
        send(line, line, gn_s.at[1, m], gn_r.at[1, m], to)

    r_iota = lax.broadcasted_iota(jnp.int32, (two, 2 * n), 0).astype(F32)
    lane = lax.broadcasted_iota(jnp.int32, (1, 2 * n), 1)
    shift = jnp.where(lane >= n, float(capacity), 0.0)
    here = (2 * E).astype(F32)

    def select(r):
        p = mod(jnp.where(r < H, z + r, z + H - 1 - r), Z)
        got(tok.at[2 * p + 1 - c], sb_s.at[r], sb_r.at[r])
        m0 = tok[2 * p, n : n + 2 * topk, :].astype(F32)
        m1 = tok[2 * p + 1, n : n + 2 * topk, :].astype(F32)

        def both(i, l):
            return jnp.concatenate(
                [
                    m0[i * topk : (i + 1) * topk, l * n : (l + 1) * n],
                    m1[i * topk : (i + 1) * topk, l * n : (l + 1) * n],
                ],
                axis=1,
            )

        idp, high, low, pos = both(0, 0), both(0, 1), both(1, 0), both(1, 1)
        picked = []
        for j in range(2):
            hit = idp == here + float(j)
            named = jnp.sum(jnp.where(hit, 1.0, 0.0), axis=0, keepdims=True)
            slot = jnp.sum(jnp.where(hit, pos, 0.0), axis=0, keepdims=True)
            wh = jnp.sum(jnp.where(hit, high, 0.0), axis=0, keepdims=True)
            wo = jnp.sum(jnp.where(hit, low, 0.0), axis=0, keepdims=True)
            slot = jnp.where(named > 0.5, slot + shift, -1.0)
            taken = jnp.where(r_iota == slot, 1.0, 0.0)
            sw[r, j * two : (j + 1) * two, :] = (taken * wh).astype(BF)
            sw[r, (2 + j) * two : (3 + j) * two, :] = (taken * wo).astype(BF)
            picked.append(taken.astype(BF))
        pair = tok[pl.ds(2 * p, 2), 0:n, :].reshape(2 * n, wide)
        taken = dot(jnp.concatenate(picked, axis=0), pair, 1, 0).astype(BF)
        rows[0, r] = taken[0:two, :]
        rows[1, r] = taken[two : 2 * two, :]

    def z_step(s, carry):
        pr, po = mod(z - 1 - s, Z), mod(z + 1 + s, Z)
        er, eo = 2 * pr + c, 2 * po + c
        for u in range(2):
            br, bo = tok.at[er, cuts[u]], tok.at[eo, cuts[u]]
            got(br, za_s.at[0, s, u], za_r.at[0, s, u])

            @pl.when(s < H - 1)
            def _():
                send(br, br, za_s.at[0, s + 1, u], za_r.at[0, s + 1, u], z_up)
                got(bo, za_s.at[1, s, u], za_r.at[1, s, u])

            @pl.when(s < H - 2)
            def _():
                send(bo, bo, za_s.at[1, s + 1, u], za_r.at[1, s + 1, u], z_down)

        send(tok.at[er], tok.at[er], sb_s.at[H + s], sb_r.at[H + s], other)

        @pl.when(s < H - 1)
        def _():
            send(tok.at[eo], tok.at[eo], sb_s.at[s + 1], sb_r.at[s + 1], other)

        select(s)

        @pl.when(s > 0)
        def _():
            select(H + s - 1)

        return carry

    lax.fori_loop(0, H, z_step, 0)
    select(Z - 1)

    def mine_of(j, ch, half):
        return rows.at[j, pl.ds(H * half + Q * ch, Q)]

    for ch in (1, 0):
        for j in range(2):
            a, b = axes(j)
            sh = b * SIDE + a
            pltpu.make_async_copy(
                mine_of(j, ch, lax.rem(a, 2)), gath.at[j, ch, sh], a_r.at[j, ch, 0]
            ).start()
            for k in (1, 3, 2):
                to = mod(a - k, SIDE)
                send(
                    mine_of(j, ch, lax.rem(to, 2)), gath.at[j, ch, sh],
                    a_s.at[j, ch, k], a_r.at[j, ch, k], device(j, to, b),
                )

    def forward(j, ch, k):
        a, b = axes(j)
        piece = gath.at[j, ch, b * SIDE + mod(a + k, SIDE)]
        for way, d in ((0, 1), (1, -1)):
            send(
                piece, piece, b_s.at[j, ch, k, way], b_r.at[j, ch, k, way],
                device(j, a, mod(b + d, SIDE)),
            )

    def near(ch):
        for j in range(2):
            a, b = axes(j)
            pltpu.make_async_copy(
                mine_of(j, ch, lax.rem(a, 2)), gath.at[j, ch, b * SIDE + a], a_r.at[j, ch, 0]
            ).wait()
            forward(j, ch, 0)

        def step(i, carry):
            j, k = lax.rem(i, 2), lax.div(i, 2)
            a, b = axes(j)
            sh = b * SIDE + mod(a + k, SIDE)
            got(gath.at[j, ch, sh], a_s.at[j, ch, k], a_r.at[j, ch, k])
            forward(j, ch, k)
            return carry

        lax.fori_loop(2, 2 * SIDE, step, 0)

    def multiply(j, ch, sh):
        piece = gath[j, ch, sh].reshape(chunk_rows, wide).astype(F32)
        ssq[j, ch] += piece * piece
        piece = (piece * gains[owner(j, sh), 0:1, :]).astype(BF)
        col = column(j, sh)
        accg[j, ch] += dot(piece, wts[j, 0, :, col], 1, 1)
        accu[j, ch] += dot(piece, wts[j, 1, :, col], 1, 1)

    def multiply_near(ch):
        def step(i, carry):
            j, k = lax.rem(i, 2), lax.div(i, 2)
            multiply(j, ch, axes(j)[1] * SIDE + k)
            return carry

        lax.fori_loop(0, 2 * SIDE, step, 0)

    def side(ch, work):
        def step(i, carry):
            j, k = lax.rem(i, 2), lax.div(i, 2)
            a, b = axes(j)
            low = mod(b - 1, SIDE) * SIDE + mod(a + k, SIDE)
            high = mod(b + 1, SIDE) * SIDE + mod(a + k, SIDE)
            got(gath.at[j, ch, low], b_s.at[j, ch, k, 0], b_r.at[j, ch, k, 0])

            @pl.when(lax.rem(k, 2) == 0)
            def _():
                piece = gath.at[j, ch, low]
                to = device(j, a, mod(b + 1, SIDE))
                send(piece, piece, f_s.at[j, ch, k], f_r.at[j, ch, k], to)

            got(gath.at[j, ch, high], b_s.at[j, ch, k, 1], b_r.at[j, ch, k, 1])

            @pl.when(lax.rem(k, 2) == 1)
            def _():
                piece = gath.at[j, ch, high]
                to = device(j, a, mod(b - 1, SIDE))
                send(piece, piece, f_s.at[j, ch, k], f_r.at[j, ch, k], to)

            if work:
                multiply(j, ch, low)
                multiply(j, ch, high)
            return carry

        lax.fori_loop(0, 2 * SIDE, step, 0)

    def multiply_side(ch):
        def step(i, carry):
            j, k = lax.rem(i, 2), lax.div(i, 2)
            b = axes(j)[1]
            multiply(j, ch, mod(b - 1, SIDE) * SIDE + k)
            multiply(j, ch, mod(b + 1, SIDE) * SIDE + k)
            return carry

        lax.fori_loop(0, 2 * SIDE, step, 0)

    def far(ch):
        def step(i, carry):
            j, k = lax.rem(i, 2), lax.div(i, 2)
            a, b = axes(j)
            sh = mod(b + 2, SIDE) * SIDE + mod(a + k, SIDE)
            got(gath.at[j, ch, sh], f_s.at[j, ch, k], f_r.at[j, ch, k])
            multiply(j, ch, sh)
            return carry

        lax.fori_loop(0, 2 * SIDE, step, 0)

    def activate(ch):
        for j in range(2):
            total = jnp.sum(ssq[j, ch], axis=1, keepdims=True)
            scale = lax.rsqrt(total / width + epsilon)
            g = accg[j, ch] * scale
            inner[j, ch] = (g / (1.0 + jnp.exp(-g)) * (accu[j, ch] * scale)).astype(BF)

    lo, hi = pl.ds(0, A), pl.ds(A, A)

    def ends(j):
        a, b = axes(j)
        return device(j, a, mod(b + 1, SIDE)), device(j, a, mod(b - 1, SIDE))

    def down(ch):
        for d in (2, 1, 3, 0):

            def step(i, carry, d=d):
                j, aa = lax.rem(i, 2), lax.div(i, 2)
                sh = mod(axes(j)[1] + d, SIDE) * SIDE + aa
                made = dot(inner[j, ch], wts[j, 2, :, column(j, sh)], 1, 0).astype(BF)
                part[j, ch, sh] = made.reshape(Q, two, wide)
                return carry

            lax.fori_loop(0, 2 * SIDE, step, 0)
            for j in range(2):
                above, below = ends(j)
                bundle = part.at[j, ch, pl.ds(mod(axes(j)[1] + d, SIDE) * SIDE, SIDE)]
                ss, rs = r1_s.at[j, ch], r1_r.at[j, ch]
                if d == 2:
                    send(bundle.at[:, lo], hop.at[j, ch, 0], ss.at[0], rs.at[0], above)
                    send(bundle.at[:, hi], hop.at[j, ch, 1], ss.at[1], rs.at[1], below)
                elif d == 1:
                    send(bundle.at[:, hi], from_l.at[j, ch, :, hi], ss.at[2], rs.at[2], above)
                elif d == 3:
                    send(bundle.at[:, lo], from_r.at[j, ch, :, lo], ss.at[3], rs.at[3], below)

    def hops(ch):
        for way, (d, cut, target) in enumerate(((1, lo, from_l), (3, hi, from_r))):
            for j in range(2):
                first = mod(axes(j)[1] + d, SIDE) * SIDE
                got(hop.at[j, ch, way], r1_s.at[j, ch, way], r1_r.at[j, ch, way])

                def step(aa, carry, j=j, first=first, cut=cut, way=way):
                    mixed = part[j, ch, first + aa, cut].astype(F32) + hop[j, ch, way, aa].astype(
                        F32
                    )
                    part[j, ch, first + aa, cut] = mixed.astype(BF)
                    return carry

                lax.fori_loop(0, SIDE, step, 0)
                send(
                    part.at[j, ch, pl.ds(first, SIDE), cut], target.at[j, ch, :, cut],
                    r2_s.at[j, ch, way], r2_r.at[j, ch, way], ends(j)[way],
                )

    def columns(ch):
        for j in range(2):
            a, b = axes(j)
            got(from_l.at[j, ch, :, hi], r1_s.at[j, ch, 2], r1_r.at[j, ch, 2])
            got(from_r.at[j, ch, :, lo], r1_s.at[j, ch, 3], r1_r.at[j, ch, 3])
            got(from_l.at[j, ch, :, lo], r2_s.at[j, ch, 0], r2_r.at[j, ch, 0])
            got(from_r.at[j, ch, :, hi], r2_s.at[j, ch, 1], r2_r.at[j, ch, 1])

            def step(i, carry, j=j, a=a, b=b):
                m = lax.rem(SIDE + 2 - i, SIDE)
                aa = mod(a + m, SIDE)
                mixed = (
                    part[j, ch, b * SIDE + aa].astype(F32)
                    + from_l[j, ch, aa].astype(F32)
                    + from_r[j, ch, aa].astype(F32)
                )
                vsum[j, ch, m] = mixed.astype(BF)

                @pl.when(m > 0)
                def _():
                    send(
                        vsum.at[j, ch, m], cross.at[j, ch, m], c_s.at[j, ch, m],
                        c_r.at[j, ch, m], device(j, aa, b),
                    )

                return carry

            lax.fori_loop(0, SIDE, step, 0)

    def finish(ch):
        for j in range(2):
            own = lax.rem(axes(j)[0], 2)
            for m in (1, 3, 2):
                got(cross.at[j, ch, m], c_s.at[j, ch, m], c_r.at[j, ch, m])
            final[j, pl.ds(H * (1 - own) + Q * ch, Q)] = (
                cross[j, ch, 1].astype(F32) + cross[j, ch, 3].astype(F32)
            ).astype(BF)
            final[j, pl.ds(H * own + Q * ch, Q)] = (
                vsum[j, ch, 0].astype(F32) + cross[j, ch, 2].astype(F32)
            ).astype(BF)

    accg[...] = jnp.zeros_like(accg)
    accu[...] = jnp.zeros_like(accu)
    ssq[...] = jnp.zeros_like(ssq)
    near(1)
    for m in range(1, SIDE):
        got(gains.at[pl.ds(mod(y - m, SIDE) * SIDE, SIDE)], gn_s.at[1, m], gn_r.at[1, m])
    for j in range(2):
        for i, w in enumerate((w_gate, w_up, w_down)):
            pltpu.make_async_copy(w.at[j], wts.at[j, i, pl.ds(0, fh)], wl_r.at[j, i]).wait()
            got(wts.at[j, i, pl.ds(fh, fh)], w_s.at[j, i], w_r.at[j, i])
    near(0)
    multiply_near(1)
    side(1, True)
    side(0, False)
    multiply_near(0)
    far(1)
    activate(1)
    down(1)
    multiply_side(0)
    far(0)
    activate(0)
    hops(1)
    down(0)

    def combine(r):
        stacked = jnp.concatenate([final[0, r], final[1, r]], axis=0)
        stacked = jnp.concatenate([stacked, stacked], axis=0)
        made = dot(sw[r], stacked, 0, 0).astype(BF)
        cont[r, 0] = made[0:n, :]
        cont[r, 1] = made[n : 2 * n, :]
        send(cont.at[r, 1 - c], sib.at[r], cs_s.at[r], cs_r.at[r], other)

    hn = n // 2

    def pass_on(way, s, r, to):
        got(sib.at[r], cs_s.at[r], cs_r.at[r])
        for u in range(2):
            cut = pl.ds(u * hn, hn)

            @pl.when(s == 0)
            def _():
                cont[r, c, cut] = (cont[r, c, cut].astype(F32) + sib[r, cut].astype(F32)).astype(BF)

            @pl.when(s > 0)
            def _():
                got(zin.at[way, s - 1, cut], q_s.at[way, s - 1, u], q_r.at[way, s - 1, u])
                cont[r, c, cut] = (
                    cont[r, c, cut].astype(F32)
                    + sib[r, cut].astype(F32)
                    + zin[way, s - 1, cut].astype(F32)
                ).astype(BF)

            send(
                cont.at[r, c, cut], zin.at[way, s, cut], q_s.at[way, s, u], q_r.at[way, s, u], to
            )

    def place_right(s):
        return jnp.where(s == 0, Z - 1, H - s)

    def ring_first(s, carry):
        @pl.when(s < Q)
        def _():
            combine(H - 1 - s)

            @pl.when(s < Q - 1)
            def _():
                combine(Z - 2 - s)

        pass_on(0, s, place_right(s), z_up)

        @pl.when((s > 0) & (s < Q))
        def _():
            pass_on(1, s - 1, Z - 1 - s, z_down)

        return carry

    def ring_last(s, carry):
        pass_on(1, s - 2, Z - s, z_down)

        @pl.when(s < H)
        def _():
            combine(H - 1 - s)
            pass_on(0, s, H - s, z_up)

        @pl.when(s < H)
        def _():
            combine(Z - 1 - s)

        return carry

    columns(1)
    finish(1)
    combine(Z - 1)
    lax.fori_loop(0, 2, ring_first, 0)
    hops(0)
    lax.fori_loop(2, Q, ring_first, 0)
    columns(0)
    lax.fori_loop(Q, Q + 1, ring_first, 0)
    finish(0)
    combine(H + Q - 1)
    combine(Q - 1)
    lax.fori_loop(Q + 1, H + 1, ring_last, 0)
    got(sib.at[0], cs_s.at[0], cs_r.at[0])
    for u in range(2):
        cut = pl.ds(u * hn, hn)
        got(zin.at[1, H - 2, cut], q_s.at[1, H - 2, u], q_r.at[1, H - 2, u])
        got(zin.at[0, H - 1, cut], q_s.at[0, H - 1, u], q_r.at[0, H - 1, u])
        out[cut] = (
            cont[0, c, cut].astype(F32)
            + sib[0, cut].astype(F32)
            + zin[1, H - 2, cut].astype(F32)
            + zin[0, H - 1, cut].astype(F32)
        ).astype(BF)

    for m in range(1, SIDE):
        left(gains.at[0], gn_s.at[0, m], gn_r.at[0, m])
        left(line, gn_s.at[1, m], gn_r.at[1, m])

    def left_z(s, carry):
        for u in range(2):
            left(tok.at[0, cuts[u]], za_s.at[0, s, u], za_r.at[0, s, u])
            cut = pl.ds(u * hn, hn)
            left(zin.at[0, 0, cut], q_s.at[0, s, u], q_r.at[0, s, u])

            @pl.when(s < H - 1)
            def _():
                left(tok.at[0, cuts[u]], za_s.at[1, s, u], za_r.at[1, s, u])
                left(zin.at[1, 0, cut], q_s.at[1, s, u], q_r.at[1, s, u])

        return carry

    lax.fori_loop(0, H, left_z, 0)

    def left_pairs(r, carry):
        left(tok.at[0], sb_s.at[r], sb_r.at[r])
        left(sib.at[0], cs_s.at[r], cs_r.at[r])
        return carry

    lax.fori_loop(0, Z, left_pairs, 0)
    for j in range(2):
        for i, w in enumerate((w_gate, w_up, w_down)):
            left(w.at[j], w_s.at[j, i], w_r.at[j, i])

    def left_pieces(i, carry):
        j, ch, k = lax.rem(i, 2), lax.rem(lax.div(i, 2), 2), lax.div(i, 4)
        piece = gath.at[j, ch, 0]

        @pl.when(k > 0)
        def _():
            left(piece, a_s.at[j, ch, k], a_r.at[j, ch, k])
            left(piece, c_s.at[j, ch, k], c_r.at[j, ch, k])

        left(piece, b_s.at[j, ch, k, 0], b_r.at[j, ch, k, 0])
        left(piece, b_s.at[j, ch, k, 1], b_r.at[j, ch, k, 1])
        left(piece, f_s.at[j, ch, k], f_r.at[j, ch, k])
        left(hop.at[j, ch, 0], r1_s.at[j, ch, k], r1_r.at[j, ch, k])

        @pl.when(k < 2)
        def _():
            left(hop.at[j, ch, 0], r2_s.at[j, ch, k], r2_r.at[j, ch, k])

        return carry

    lax.fori_loop(0, 4 * SIDE, left_pieces, 0)


def body(hidden_in, norm_gain, expert_ids, route_weights, w_gate, w_up, w_down):
    n, wide = hidden_in.shape
    topk = expert_ids.shape[1]
    fh = w_gate.shape[1]
    groups = lax.axis_size("expert")
    Z = groups // 2
    H, Q = Z // 2, Z // 4
    capacity = min(n, 3 * n * topk // (2 * 2 * groups))
    two = 2 * capacity
    vm, dma = pltpu.VMEM, pltpu.SemaphoreType.DMA
    shards = SIDE * SIDE
    scratch = [
        vm((groups, n + 2 * topk, wide), BF),
        vm((2, Z, two, wide), BF),
        vm((2, 2, shards, Q, two, wide), BF),
        vm((2, 3, 2 * fh, shards * wide), BF),
        vm((2, 2, Q * two, 2 * fh), F32),
        vm((2, 2, Q * two, 2 * fh), F32),
        vm((2, 2, Q * two, wide), F32),
        vm((2, 2, Q * two, 2 * fh), BF),
        vm((2, 2, shards, Q, two, wide), BF),
        vm((2, 2, 2, SIDE, Q // 2, two, wide), BF),
        vm((2, 2, SIDE, Q, two, wide), BF),
        vm((2, 2, SIDE, Q, two, wide), BF),
        vm((2, 2, SIDE, Q, two, wide), BF),
        vm((2, 2, SIDE, Q, two, wide), BF),
        vm((2, Z, two, wide), BF),
        vm((Z, 4 * two, 2 * n), BF),
        vm((Z, 2, n, wide), BF),
        vm((Z, n, wide), BF),
        vm((2, H, n, wide), BF),
        vm((shards, 8, wide), F32),
        dma((2, SIDE)), dma((2, SIDE)),
        dma((2, H, 2)), dma((2, H, 2)),
        dma((Z,)), dma((Z,)),
        dma((2, 3)), dma((2, 3)), dma((2, 3)),
        dma((2, 2, SIDE)), dma((2, 2, SIDE)),
        dma((2, 2, SIDE, 2)), dma((2, 2, SIDE, 2)),
        dma((2, 2, SIDE)), dma((2, 2, SIDE)),
        dma((2, 2, SIDE)), dma((2, 2, SIDE)),
        dma((2, 2, 2)), dma((2, 2, 2)),
        dma((2, 2, SIDE)), dma((2, 2, SIDE)),
        dma((Z,)), dma((Z,)),
        dma((2, H, 2)), dma((2, H, 2)),
    ]
    vmem = pl.BlockSpec(memory_space=pltpu.VMEM)
    anywhere = pl.BlockSpec(memory_space=pl.ANY)
    return pl.pallas_call(
        functools.partial(kernel, Z, capacity, wide * shards),
        out_shape=jax.ShapeDtypeStruct((n, wide), BF),
        in_specs=[vmem, vmem, vmem, vmem, anywhere, anywhere, anywhere],
        out_specs=vmem,
        scratch_shapes=scratch,
        compiler_params=pltpu.CompilerParams(
            collective_id=0, has_side_effects=True, vmem_limit_bytes=58 * 2**20
        ),
    )(hidden_in, norm_gain[None, :], expert_ids, route_weights, w_gate, w_up, w_down)


def solution(mesh):
    placed = (
        P("expert", "tensor"),
        P("tensor"),
        P("expert", None),
        P("expert", None),
        P("expert", "tensor", None),
        P("expert", "tensor", None),
        P("expert", "tensor", None),
    )
    return jax.shard_map(
        body, mesh=mesh, in_specs=placed, out_specs=P("expert", "tensor"), check_vma=False
    )
```

```python
import functools

import jax
import jax.numpy as jnp
from jax import lax
from jax.experimental import pallas as pl
from jax.experimental.pallas import tpu as pltpu
from jax.sharding import PartitionSpec as P

epsilon = 1e-06
SIDE = 4
BF = jnp.bfloat16
F32 = jnp.float32


def dot(a, b, ca, cb):
    return lax.dot_general(a, b, (((ca,), (cb,)), ((), ())), preferred_element_type=F32)


def kernel(
    Z, capacity, width,
    hid, gain, ids_in, weights_in, w_gate, w_up, w_down, out,
    tok, rows, gath, wts, accg, accu, ssq, inner, part, hop, from_l, from_r, vsum, cross, final,
    sw, cont, sib, zin, gains,
    gn_s, gn_r, za_s, za_r, sb_s, sb_r, wl_r, w_s, w_r, a_s, a_r, b_s, b_r, f_s, f_r,
    r1_s, r1_r, r2_s, r2_r, c_s, c_r, cs_s, cs_r, q_s, q_r,
):
    H = Z // 2
    Q = H // 2
    A = Q // 4
    n, wide = hid.shape
    fh = w_gate.shape[1]
    topk = ids_in.shape[1]
    experts = 4 * Z
    two = 2 * capacity
    chunk_rows = Q * two
    mesh_ids = pl.DeviceIdType.MESH

    E = lax.axis_index("expert")
    T = lax.axis_index("tensor")
    z, c = lax.div(E, 2), lax.rem(E, 2)
    y, x = lax.div(T, SIDE), lax.rem(T, SIDE)

    def mod(v, m):
        return lax.rem(v + m, m)

    def axes(j):
        return (x + j * (y - x), y + j * (x - y))

    def device(j, a, b):
        return (E, (b + j * (a - b)) * SIDE + a + j * (b - a))

    def owner(j, sh):
        bb, aa = lax.div(sh, SIDE), lax.rem(sh, SIDE)
        return bb * SIDE + aa + j * (aa * SIDE + bb - bb * SIDE - aa)

    def column(j, sh):
        return pl.ds(pl.multiple_of(owner(j, sh) * wide, wide), wide)

    def send(src, dst, ssem, rsem, to):
        pltpu.make_async_remote_copy(
            src_ref=src, dst_ref=dst, send_sem=ssem, recv_sem=rsem,
            device_id=to, device_id_type=mesh_ids,
        ).start()

    def got(dst, ssem, rsem):
        pltpu.make_async_remote_copy(
            src_ref=dst, dst_ref=dst, send_sem=ssem, recv_sem=rsem,
            device_id=(E, T), device_id_type=mesh_ids,
        ).wait_recv()

    def left(src, ssem, rsem):
        pltpu.make_async_remote_copy(
            src_ref=src, dst_ref=src, send_sem=ssem, recv_sem=rsem,
            device_id=(E, T), device_id_type=mesh_ids,
        ).wait_send()

    other = (2 * z + 1 - c, T)
    z_up = (2 * mod(z + 1, Z) + c, T)
    z_down = (2 * mod(z - 1, Z) + c, T)

    barrier = pltpu.get_barrier_semaphore()
    partners = [other, z_up, z_down]
    for m in range(1, SIDE):
        partners.append((E, y * SIDE + mod(x + m, SIDE)))
        partners.append((E, mod(y + m, SIDE) * SIDE + x))
    for partner in partners:
        pl.semaphore_signal(barrier, inc=1, device_id=partner, device_id_type=mesh_ids)

    ids = ids_in[...].astype(F32).T
    wts_t = weights_in[...].T
    e_iota = lax.broadcasted_iota(jnp.int32, (experts, n), 0).astype(F32)
    hits = [e_iota == ids[k : k + 1, :] for k in range(topk)]
    chosen = jnp.zeros((experts, n), F32)
    for k in range(topk):
        chosen = chosen + jnp.where(hits[k], 1.0, 0.0)
    tri = (
        lax.broadcasted_iota(jnp.int32, (n, n), 0) < lax.broadcasted_iota(jnp.int32, (n, n), 1)
    ).astype(F32).astype(BF)
    before = dot(chosen.astype(BF), tri, 1, 0)
    pos = jnp.concatenate(
        [jnp.sum(jnp.where(hits[k], before, 0.0), axis=0, keepdims=True) for k in range(topk)],
        axis=0,
    )
    high = wts_t.astype(BF).astype(F32)
    meta = jnp.concatenate(
        [jnp.concatenate([ids, high], axis=1), jnp.concatenate([wts_t - high, pos], axis=1)],
        axis=0,
    )
    tok[E, n : n + 2 * topk, :] = meta.astype(BF)
    tok[E, 0:n, :] = hid[...]
    gains[T] = jnp.broadcast_to(gain[...], (8, wide))
    for j in range(2):
        for i, w in enumerate((w_gate, w_up, w_down)):
            pltpu.make_async_copy(w.at[j], wts.at[j, i, pl.ds(0, fh)], wl_r.at[j, i]).start()
    pl.semaphore_wait(barrier, len(partners))

    nb = 16 * ((n + 2 * topk + 31) // 32)
    cuts = [pl.ds(0, nb), pl.ds(nb, n + 2 * topk - nb)]
    for u in range(2):
        mine = tok.at[E, cuts[u]]
        send(mine, mine, za_s.at[0, 0, u], za_r.at[0, 0, u], z_up)
        send(mine, mine, za_s.at[1, 0, u], za_r.at[1, 0, u], z_down)
    send(tok.at[E], tok.at[E], sb_s.at[0], sb_r.at[0], other)
    for m in range(1, SIDE):
        to = (E, y * SIDE + mod(x + m, SIDE))
        send(gains.at[T], gains.at[T], gn_s.at[0, m], gn_r.at[0, m], to)

    for i, w in enumerate((w_gate, w_up, w_down)):
        for j in range(2):
            a, b = axes(j)
            mate = mod(a + 1 - 2 * lax.rem(a + c, 2), SIDE)
            send(w.at[j], wts.at[j, i, pl.ds(fh, fh)], w_s.at[j, i], w_r.at[j, i], device(j, mate, b))

    r_iota = lax.broadcasted_iota(jnp.int32, (two, 2 * n), 0).astype(F32)
    lane = lax.broadcasted_iota(jnp.int32, (1, 2 * n), 1)
    shift = jnp.where(lane >= n, float(capacity), 0.0)
    here = (2 * E).astype(F32)

    def select(r):
        p = mod(jnp.where(r < H, z + r, z + H - 1 - r), Z)
        got(tok.at[2 * p + 1 - c], sb_s.at[r], sb_r.at[r])
        m0 = tok[2 * p, n : n + 2 * topk, :].astype(F32)
        m1 = tok[2 * p + 1, n : n + 2 * topk, :].astype(F32)

        def both(i, l):
            return jnp.concatenate(
                [
                    m0[i * topk : (i + 1) * topk, l * n : (l + 1) * n],
                    m1[i * topk : (i + 1) * topk, l * n : (l + 1) * n],
                ],
                axis=1,
            )

        idp, high, low, pos = both(0, 0), both(0, 1), both(1, 0), both(1, 1)
        picked = []
        for j in range(2):
            hit = idp == here + float(j)
            named = jnp.sum(jnp.where(hit, 1.0, 0.0), axis=0, keepdims=True)
            slot = jnp.sum(jnp.where(hit, pos, 0.0), axis=0, keepdims=True)
            wh = jnp.sum(jnp.where(hit, high, 0.0), axis=0, keepdims=True)
            wo = jnp.sum(jnp.where(hit, low, 0.0), axis=0, keepdims=True)
            slot = jnp.where(named > 0.5, slot + shift, -1.0)
            taken = jnp.where(r_iota == slot, 1.0, 0.0)
            sw[r, j * two : (j + 1) * two, :] = (taken * wh).astype(BF)
            sw[r, (2 + j) * two : (3 + j) * two, :] = (taken * wo).astype(BF)
            picked.append(taken.astype(BF))
        pair = tok[pl.ds(2 * p, 2), 0:n, :].reshape(2 * n, wide)
        taken = dot(jnp.concatenate(picked, axis=0), pair, 1, 0).astype(BF)
        rows[0, r] = taken[0:two, :]
        rows[1, r] = taken[two : 2 * two, :]

    def z_step(s, carry):
        pr, po = mod(z - 1 - s, Z), mod(z + 1 + s, Z)
        er, eo = 2 * pr + c, 2 * po + c
        for u in range(2):
            br, bo = tok.at[er, cuts[u]], tok.at[eo, cuts[u]]
            got(br, za_s.at[0, s, u], za_r.at[0, s, u])

            @pl.when(s < H - 1)
            def _():
                send(br, br, za_s.at[0, s + 1, u], za_r.at[0, s + 1, u], z_up)
                got(bo, za_s.at[1, s, u], za_r.at[1, s, u])

            @pl.when(s < H - 2)
            def _():
                send(bo, bo, za_s.at[1, s + 1, u], za_r.at[1, s + 1, u], z_down)

        send(tok.at[er], tok.at[er], sb_s.at[H + s], sb_r.at[H + s], other)

        @pl.when(s < H - 1)
        def _():
            send(tok.at[eo], tok.at[eo], sb_s.at[s + 1], sb_r.at[s + 1], other)

        select(s)

        @pl.when(s > 0)
        def _():
            select(H + s - 1)

        return carry

    def mine_of(j, ch, half):
        return rows.at[j, pl.ds(H * half + Q * ch, Q)]

    def scatter(ch):
        for j in range(2):
            a, b = axes(j)
            sh = b * SIDE + a
            pltpu.make_async_copy(
                mine_of(j, ch, lax.rem(a, 2)), gath.at[j, ch, sh], a_r.at[j, ch, 0]
            ).start()
            for k in (1, 3, 2):
                to = mod(a - k, SIDE)
                send(
                    mine_of(j, ch, lax.rem(to, 2)), gath.at[j, ch, sh],
                    a_s.at[j, ch, k], a_r.at[j, ch, k], device(j, to, b),
                )

    lax.fori_loop(0, Q + 1, z_step, 0)
    scatter(0)
    for m in range(1, SIDE):
        got(gains.at[y * SIDE + mod(x - m, SIDE)], gn_s.at[0, m], gn_r.at[0, m])
    line = gains.at[pl.ds(y * SIDE, SIDE)]
    for m in range(1, SIDE):
        to = (E, mod(y + m, SIDE) * SIDE + x)
        send(line, line, gn_s.at[1, m], gn_r.at[1, m], to)
    lax.fori_loop(Q + 1, H, z_step, 0)
    select(Z - 1)
    scatter(1)

    def forward(j, ch, k):
        a, b = axes(j)
        piece = gath.at[j, ch, b * SIDE + mod(a + k, SIDE)]
        for way, d in ((0, 1), (1, -1)):
            send(
                piece, piece, b_s.at[j, ch, k, way], b_r.at[j, ch, k, way],
                device(j, a, mod(b + d, SIDE)),
            )

    def near(ch):
        for j in range(2):
            a, b = axes(j)
            pltpu.make_async_copy(
                mine_of(j, ch, lax.rem(a, 2)), gath.at[j, ch, b * SIDE + a], a_r.at[j, ch, 0]
            ).wait()
            forward(j, ch, 0)

        def step(i, carry):
            j, k = lax.rem(i, 2), lax.div(i, 2)
            a, b = axes(j)
            sh = b * SIDE + mod(a + k, SIDE)
            got(gath.at[j, ch, sh], a_s.at[j, ch, k], a_r.at[j, ch, k])
            forward(j, ch, k)
            return carry

        lax.fori_loop(2, 2 * SIDE, step, 0)

    def multiply(j, ch, sh):
        piece = gath[j, ch, sh].reshape(chunk_rows, wide).astype(F32)
        ssq[j, ch] += piece * piece
        piece = (piece * gains[owner(j, sh), 0:1, :]).astype(BF)
        col = column(j, sh)
        accg[j, ch] += dot(piece, wts[j, 0, :, col], 1, 1)
        accu[j, ch] += dot(piece, wts[j, 1, :, col], 1, 1)

    def multiply_near(ch):
        def step(i, carry):
            j, k = lax.rem(i, 2), lax.div(i, 2)
            multiply(j, ch, axes(j)[1] * SIDE + k)
            return carry

        lax.fori_loop(0, 2 * SIDE, step, 0)

    def side(ch, work):
        def step(i, carry):
            j, k = lax.rem(i, 2), lax.div(i, 2)
            a, b = axes(j)
            low = mod(b - 1, SIDE) * SIDE + mod(a + k, SIDE)
            high = mod(b + 1, SIDE) * SIDE + mod(a + k, SIDE)
            got(gath.at[j, ch, low], b_s.at[j, ch, k, 0], b_r.at[j, ch, k, 0])

            @pl.when(lax.rem(k, 2) == 0)
            def _():
                piece = gath.at[j, ch, low]
                to = device(j, a, mod(b + 1, SIDE))
                send(piece, piece, f_s.at[j, ch, k], f_r.at[j, ch, k], to)

            got(gath.at[j, ch, high], b_s.at[j, ch, k, 1], b_r.at[j, ch, k, 1])

            @pl.when(lax.rem(k, 2) == 1)
            def _():
                piece = gath.at[j, ch, high]
                to = device(j, a, mod(b - 1, SIDE))
                send(piece, piece, f_s.at[j, ch, k], f_r.at[j, ch, k], to)

            if work:
                multiply(j, ch, low)
                multiply(j, ch, high)
            return carry

        lax.fori_loop(0, 2 * SIDE, step, 0)

    def multiply_side(ch):
        def step(i, carry):
            j, k = lax.rem(i, 2), lax.div(i, 2)
            b = axes(j)[1]
            multiply(j, ch, mod(b - 1, SIDE) * SIDE + k)
            multiply(j, ch, mod(b + 1, SIDE) * SIDE + k)
            return carry

        lax.fori_loop(0, 2 * SIDE, step, 0)

    def far(ch):
        def step(i, carry):
            j, k = lax.rem(i, 2), lax.div(i, 2)
            a, b = axes(j)
            sh = mod(b + 2, SIDE) * SIDE + mod(a + k, SIDE)
            got(gath.at[j, ch, sh], f_s.at[j, ch, k], f_r.at[j, ch, k])
            multiply(j, ch, sh)
            return carry

        lax.fori_loop(0, 2 * SIDE, step, 0)

    def activate(ch):
        for j in range(2):
            total = jnp.sum(ssq[j, ch], axis=1, keepdims=True)
            scale = lax.rsqrt(total / width + epsilon)
            g = accg[j, ch] * scale
            inner[j, ch] = (g / (1.0 + jnp.exp(-g)) * (accu[j, ch] * scale)).astype(BF)

    def cuts_of(rc):
        first = 2 * A * (rc % 2)
        return pl.ds(first, A), pl.ds(first + A, A), pl.ds(first, 2 * A)

    def ends(j):
        a, b = axes(j)
        return device(j, a, mod(b + 1, SIDE)), device(j, a, mod(b - 1, SIDE))

    def hand_out(rc, d):
        ch, (lo, hi, _) = rc // 2, cuts_of(rc)
        slot = pl.ds(A * (rc % 2), A)
        for j in range(2):
            above, below = ends(j)
            bundle = part.at[j, ch, pl.ds(mod(axes(j)[1] + d, SIDE) * SIDE, SIDE)]
            ss, rs = r1_s.at[j, rc], r1_r.at[j, rc]
            if d == 2:
                send(bundle.at[:, lo], hop.at[j, ch, 0, :, slot], ss.at[0], rs.at[0], above)
                send(bundle.at[:, hi], hop.at[j, ch, 1, :, slot], ss.at[1], rs.at[1], below)
            elif d == 1:
                send(bundle.at[:, hi], from_l.at[j, ch, :, hi], ss.at[2], rs.at[2], above)
            elif d == 3:
                send(bundle.at[:, lo], from_r.at[j, ch, :, lo], ss.at[3], rs.at[3], below)

    def down(ch, d):
        def step(i, carry):
            j, aa = lax.rem(i, 2), lax.div(i, 2)
            sh = mod(axes(j)[1] + d, SIDE) * SIDE + aa
            made = dot(inner[j, ch], wts[j, 2, :, column(j, sh)], 1, 0).astype(BF)
            part[j, ch, sh] = made.reshape(Q, two, wide)
            return carry

        lax.fori_loop(0, 2 * SIDE, step, 0)

    def hops(rc):
        ch, (lo, hi, _) = rc // 2, cuts_of(rc)
        slot = pl.ds(A * (rc % 2), A)
        for way, (d, cut, target) in enumerate(((1, lo, from_l), (3, hi, from_r))):
            for j in range(2):
                first = mod(axes(j)[1] + d, SIDE) * SIDE
                here_hop = hop.at[j, ch, way, :, slot]
                got(here_hop, r1_s.at[j, rc, way], r1_r.at[j, rc, way])
                mine_part = part.at[j, ch, pl.ds(first, SIDE), cut]
                mine_part[...] = (mine_part[...].astype(F32) + here_hop[...].astype(F32)).astype(BF)
                send(
                    mine_part, target.at[j, ch, :, cut],
                    r2_s.at[j, rc, way], r2_r.at[j, rc, way], ends(j)[way],
                )

    def columns(rc):
        ch, (lo, hi, whole) = rc // 2, cuts_of(rc)
        for j in range(2):
            a, b = axes(j)
            got(from_l.at[j, ch, :, hi], r1_s.at[j, rc, 2], r1_r.at[j, rc, 2])
            got(from_r.at[j, ch, :, lo], r1_s.at[j, rc, 3], r1_r.at[j, rc, 3])
            got(from_l.at[j, ch, :, lo], r2_s.at[j, rc, 0], r2_r.at[j, rc, 0])
            got(from_r.at[j, ch, :, hi], r2_s.at[j, rc, 1], r2_r.at[j, rc, 1])

            def step(i, carry, j=j, a=a, b=b):
                m = lax.rem(SIDE + 2 - i, SIDE)
                aa = mod(a + m, SIDE)
                mixed = (
                    part[j, ch, b * SIDE + aa, whole].astype(F32)
                    + from_l[j, ch, aa, whole].astype(F32)
                    + from_r[j, ch, aa, whole].astype(F32)
                )
                vsum[j, ch, m, whole] = mixed.astype(BF)

                @pl.when(m > 0)
                def _():
                    send(
                        vsum.at[j, ch, m, whole], cross.at[j, ch, m, whole], c_s.at[j, rc, m],
                        c_r.at[j, rc, m], device(j, aa, b),
                    )

                return carry

            lax.fori_loop(0, SIDE, step, 0)

    def finish(rc):
        ch, (_, _, whole) = rc // 2, cuts_of(rc)
        for j in range(2):
            own = lax.rem(axes(j)[0], 2)
            for m in (1, 3, 2):
                got(cross.at[j, ch, m, whole], c_s.at[j, rc, m], c_r.at[j, rc, m])
            final[j, pl.ds(H * (1 - own) + 2 * A * rc, 2 * A)] = (
                cross[j, ch, 1, whole].astype(F32) + cross[j, ch, 3, whole].astype(F32)
            ).astype(BF)
            final[j, pl.ds(H * own + 2 * A * rc, 2 * A)] = (
                vsum[j, ch, 0, whole].astype(F32) + cross[j, ch, 2, whole].astype(F32)
            ).astype(BF)

        def step(i, carry):
            combine(2 * A * (rc + 1) - 1 - lax.div(i, 2) + H * lax.rem(i + 1, 2))
            return carry

        lax.fori_loop(0, 4 * A, step, 0)

    def combine(r):
        stacked = jnp.concatenate([final[0, r], final[1, r]], axis=0)
        stacked = jnp.concatenate([stacked, stacked], axis=0)
        made = dot(sw[r], stacked, 0, 0).astype(BF)
        cont[r, 0] = made[0:n, :]
        cont[r, 1] = made[n : 2 * n, :]
        send(cont.at[r, 1 - c], sib.at[r], cs_s.at[r], cs_r.at[r], other)

    hn = n // 2

    def pass_on(way, s, r, to):
        got(sib.at[r], cs_s.at[r], cs_r.at[r])
        for u in range(2):
            cut = pl.ds(u * hn, hn)
            mixed = cont[r, c, cut].astype(F32) + sib[r, cut].astype(F32)
            if s:
                got(zin.at[way, s - 1, cut], q_s.at[way, s - 1, u], q_r.at[way, s - 1, u])
                mixed = mixed + zin[way, s - 1, cut].astype(F32)
            cont[r, c, cut] = mixed.astype(BF)
            send(
                cont.at[r, c, cut], zin.at[way, s, cut], q_s.at[way, s, u], q_r.at[way, s, u], to
            )

    def right(s):
        pass_on(0, s, Z - 1 if s == 0 else H - s, z_up)

    def leftward(s):
        pass_on(1, s, Z - 2 - s, z_down)

    accg[...] = jnp.zeros_like(accg)
    accu[...] = jnp.zeros_like(accu)
    ssq[...] = jnp.zeros_like(ssq)
    near(1)
    for m in range(1, SIDE):
        got(gains.at[pl.ds(mod(y - m, SIDE) * SIDE, SIDE)], gn_s.at[1, m], gn_r.at[1, m])

    def weights_here(kinds):
        for i in kinds:
            for j in range(2):
                w = (w_gate, w_up, w_down)[i]
                pltpu.make_async_copy(w.at[j], wts.at[j, i, pl.ds(0, fh)], wl_r.at[j, i]).wait()
                got(wts.at[j, i, pl.ds(fh, fh)], w_s.at[j, i], w_r.at[j, i])

    near(0)
    weights_here((0, 1, 2))
    multiply_near(1)
    side(1, True)
    side(0, True)
    multiply_near(0)
    far(1)
    activate(1)
    for d in (2, 1, 3, 0):
        down(1, d)
        hand_out(3, d)
        hand_out(2, d)
    far(0)
    activate(0)
    hops(3)
    down(0, 2)
    down(0, 1)
    hops(2)
    down(0, 3)
    for d in (2, 1, 3):
        hand_out(1, d)
    columns(3)
    down(0, 0)
    for d in (2, 1, 3):
        hand_out(0, d)
    columns(2)
    finish(3)
    right(0)
    hops(1)
    right(1)
    leftward(0)
    finish(2)
    hops(0)
    right(2)
    columns(1)
    right(3)
    leftward(1)
    finish(1)
    columns(0)
    right(4)
    leftward(2)
    right(5)
    leftward(3)
    finish(0)
    right(6)
    leftward(4)
    right(7)
    leftward(5)
    leftward(6)
    got(sib.at[0], cs_s.at[0], cs_r.at[0])
    for u in range(2):
        cut = pl.ds(u * hn, hn)
        got(zin.at[1, H - 2, cut], q_s.at[1, H - 2, u], q_r.at[1, H - 2, u])
        got(zin.at[0, H - 1, cut], q_s.at[0, H - 1, u], q_r.at[0, H - 1, u])
        out[cut] = (
            cont[0, c, cut].astype(F32)
            + sib[0, cut].astype(F32)
            + zin[1, H - 2, cut].astype(F32)
            + zin[0, H - 1, cut].astype(F32)
        ).astype(BF)

    for m in range(1, SIDE):
        left(gains.at[0], gn_s.at[0, m], gn_r.at[0, m])
        left(line, gn_s.at[1, m], gn_r.at[1, m])

    def left_z(s, carry):
        for u in range(2):
            left(tok.at[0, cuts[u]], za_s.at[0, s, u], za_r.at[0, s, u])
            cut = pl.ds(u * hn, hn)
            left(zin.at[0, 0, cut], q_s.at[0, s, u], q_r.at[0, s, u])

            @pl.when(s < H - 1)
            def _():
                left(tok.at[0, cuts[u]], za_s.at[1, s, u], za_r.at[1, s, u])
                left(zin.at[1, 0, cut], q_s.at[1, s, u], q_r.at[1, s, u])

        return carry

    lax.fori_loop(0, H, left_z, 0)

    def left_pairs(r, carry):
        left(tok.at[0], sb_s.at[r], sb_r.at[r])
        left(sib.at[0], cs_s.at[r], cs_r.at[r])
        return carry

    lax.fori_loop(0, Z, left_pairs, 0)
    for j in range(2):
        for i, w in enumerate((w_gate, w_up, w_down)):
            left(w.at[j], w_s.at[j, i], w_r.at[j, i])

    def left_pieces(i, carry):
        j, ch, k = lax.rem(i, 2), lax.rem(lax.div(i, 2), 2), lax.div(i, 4)
        piece = gath.at[j, ch, 0]

        @pl.when(k > 0)
        def _():
            left(piece, a_s.at[j, ch, k], a_r.at[j, ch, k])

        left(piece, b_s.at[j, ch, k, 0], b_r.at[j, ch, k, 0])
        left(piece, b_s.at[j, ch, k, 1], b_r.at[j, ch, k, 1])
        left(piece, f_s.at[j, ch, k], f_r.at[j, ch, k])
        return carry

    lax.fori_loop(0, 4 * SIDE, left_pieces, 0)

    def left_parts(i, carry):
        j, rc = lax.rem(i, 2), lax.div(i, 2)
        for k in range(SIDE):
            left(hop.at[0, 0, 0, :, pl.ds(0, A)], r1_s.at[j, rc, k], r1_r.at[j, rc, k])
            if k:
                left(cross.at[0, 0, 0, pl.ds(0, 2 * A)], c_s.at[j, rc, k], c_r.at[j, rc, k])
            if k < 2:
                left(hop.at[0, 0, 0, :, pl.ds(0, A)], r2_s.at[j, rc, k], r2_r.at[j, rc, k])
        return carry

    lax.fori_loop(0, 8, left_parts, 0)


def body(hidden_in, norm_gain, expert_ids, route_weights, w_gate, w_up, w_down):
    n, wide = hidden_in.shape
    topk = expert_ids.shape[1]
    fh = w_gate.shape[1]
    groups = lax.axis_size("expert")
    Z = groups // 2
    H, Q = Z // 2, Z // 4
    capacity = min(n, 3 * n * topk // (2 * 2 * groups))
    two = 2 * capacity
    vm, dma = pltpu.VMEM, pltpu.SemaphoreType.DMA
    shards = SIDE * SIDE
    scratch = [
        vm((groups, n + 2 * topk, wide), BF),
        vm((2, Z, two, wide), BF),
        vm((2, 2, shards, Q, two, wide), BF),
        vm((2, 3, 2 * fh, shards * wide), BF),
        vm((2, 2, Q * two, 2 * fh), F32),
        vm((2, 2, Q * two, 2 * fh), F32),
        vm((2, 2, Q * two, wide), F32),
        vm((2, 2, Q * two, 2 * fh), BF),
        vm((2, 2, shards, Q, two, wide), BF),
        vm((2, 2, 2, SIDE, Q // 2, two, wide), BF),
        vm((2, 2, SIDE, Q, two, wide), BF),
        vm((2, 2, SIDE, Q, two, wide), BF),
        vm((2, 2, SIDE, Q, two, wide), BF),
        vm((2, 2, SIDE, Q, two, wide), BF),
        vm((2, Z, two, wide), BF),
        vm((Z, 4 * two, 2 * n), BF),
        vm((Z, 2, n, wide), BF),
        vm((Z, n, wide), BF),
        vm((2, H, n, wide), BF),
        vm((shards, 8, wide), F32),
        dma((2, SIDE)), dma((2, SIDE)),
        dma((2, H, 2)), dma((2, H, 2)),
        dma((Z,)), dma((Z,)),
        dma((2, 3)), dma((2, 3)), dma((2, 3)),
        dma((2, 2, SIDE)), dma((2, 2, SIDE)),
        dma((2, 2, SIDE, 2)), dma((2, 2, SIDE, 2)),
        dma((2, 2, SIDE)), dma((2, 2, SIDE)),
        dma((2, 4, SIDE)), dma((2, 4, SIDE)),
        dma((2, 4, 2)), dma((2, 4, 2)),
        dma((2, 4, SIDE)), dma((2, 4, SIDE)),
        dma((Z,)), dma((Z,)),
        dma((2, H, 2)), dma((2, H, 2)),
    ]
    vmem = pl.BlockSpec(memory_space=pltpu.VMEM)
    anywhere = pl.BlockSpec(memory_space=pl.ANY)
    return pl.pallas_call(
        functools.partial(kernel, Z, capacity, wide * shards),
        out_shape=jax.ShapeDtypeStruct((n, wide), BF),
        in_specs=[vmem, vmem, vmem, vmem, anywhere, anywhere, anywhere],
        out_specs=vmem,
        scratch_shapes=scratch,
        compiler_params=pltpu.CompilerParams(
            collective_id=0, has_side_effects=True, vmem_limit_bytes=58 * 2**20
        ),
    )(hidden_in, norm_gain[None, :], expert_ids, route_weights, w_gate, w_up, w_down)


def solution(mesh):
    placed = (
        P("expert", "tensor"),
        P("tensor"),
        P("expert", None),
        P("expert", None),
        P("expert", "tensor", None),
        P("expert", "tensor", None),
        P("expert", "tensor", None),
    )
    return jax.shard_map(
        body, mesh=mesh, in_specs=placed, out_specs=P("expert", "tensor"), check_vma=False
    )
```

```python
import functools

import jax
import jax.numpy as jnp
from jax import lax
from jax.experimental import pallas as pl
from jax.experimental.pallas import tpu as pltpu
from jax.sharding import PartitionSpec as P

epsilon = 1e-06
SIDE = 4
BF = jnp.bfloat16
F32 = jnp.float32


def dot(a, b, ca, cb):
    return lax.dot_general(a, b, (((ca,), (cb,)), ((), ())), preferred_element_type=F32)


def kernel(
    Z, capacity, width,
    hid, gain, ids_in, weights_in, w_gate, w_up, w_down, out,
    tok, rows, gath, wts, accg, accu, ssq, inner, part, hop, from_l, from_r, vsum, cross, final,
    sw, cont, sib, zin, gains,
    gn_s, gn_r, za_s, za_r, sb_s, sb_r, wl_r, w_s, w_r, a_s, a_r, b_s, b_r, f_s, f_r,
    r1_s, r1_r, r2_s, r2_r, c_s, c_r, cs_s, cs_r, q_s, q_r,
):
    H = Z // 2
    Q = H // 2
    A = Q // 4
    n, wide = hid.shape
    fh = w_gate.shape[1]
    topk = ids_in.shape[1]
    experts = 4 * Z
    two = 2 * capacity
    chunk_rows = Q * two
    mesh_ids = pl.DeviceIdType.MESH

    E = lax.axis_index("expert")
    T = lax.axis_index("tensor")
    z, c = lax.div(E, 2), lax.rem(E, 2)
    y, x = lax.div(T, SIDE), lax.rem(T, SIDE)

    def mod(v, m):
        return lax.rem(v + m, m)

    def axes(j):
        return (x + j * (y - x), y + j * (x - y))

    def device(j, a, b):
        return (E, (b + j * (a - b)) * SIDE + a + j * (b - a))

    def owner(j, sh):
        bb, aa = lax.div(sh, SIDE), lax.rem(sh, SIDE)
        return bb * SIDE + aa + j * (aa * SIDE + bb - bb * SIDE - aa)

    def column(j, sh):
        return pl.ds(pl.multiple_of(owner(j, sh) * wide, wide), wide)

    def send(src, dst, ssem, rsem, to):
        pltpu.make_async_remote_copy(
            src_ref=src, dst_ref=dst, send_sem=ssem, recv_sem=rsem,
            device_id=to, device_id_type=mesh_ids,
        ).start()

    def got(dst, ssem, rsem):
        pltpu.make_async_remote_copy(
            src_ref=dst, dst_ref=dst, send_sem=ssem, recv_sem=rsem,
            device_id=(E, T), device_id_type=mesh_ids,
        ).wait_recv()

    def left(src, ssem, rsem):
        pltpu.make_async_remote_copy(
            src_ref=src, dst_ref=src, send_sem=ssem, recv_sem=rsem,
            device_id=(E, T), device_id_type=mesh_ids,
        ).wait_send()

    other = (2 * z + 1 - c, T)
    z_up = (2 * mod(z + 1, Z) + c, T)
    z_down = (2 * mod(z - 1, Z) + c, T)

    barrier = pltpu.get_barrier_semaphore()
    partners = [other, z_up, z_down]
    for m in range(1, SIDE):
        partners.append((E, y * SIDE + mod(x + m, SIDE)))
        partners.append((E, mod(y + m, SIDE) * SIDE + x))
    for partner in partners:
        pl.semaphore_signal(barrier, inc=1, device_id=partner, device_id_type=mesh_ids)

    ids = ids_in[...].astype(F32).T
    wts_t = weights_in[...].T
    e_iota = lax.broadcasted_iota(jnp.int32, (experts, n), 0).astype(F32)
    hits = [e_iota == ids[k : k + 1, :] for k in range(topk)]
    chosen = jnp.zeros((experts, n), F32)
    for k in range(topk):
        chosen = chosen + jnp.where(hits[k], 1.0, 0.0)
    tri = (
        lax.broadcasted_iota(jnp.int32, (n, n), 0) < lax.broadcasted_iota(jnp.int32, (n, n), 1)
    ).astype(F32).astype(BF)
    before = dot(chosen.astype(BF), tri, 1, 0)
    pos = jnp.concatenate(
        [jnp.sum(jnp.where(hits[k], before, 0.0), axis=0, keepdims=True) for k in range(topk)],
        axis=0,
    )
    high = wts_t.astype(BF).astype(F32)
    meta = jnp.concatenate(
        [jnp.concatenate([ids, high], axis=1), jnp.concatenate([wts_t - high, pos], axis=1)],
        axis=0,
    )
    tok[E, n : n + 2 * topk, :] = meta.astype(BF)
    tok[E, 0:n, :] = hid[...]
    gains[T] = jnp.broadcast_to(gain[...], (8, wide))
    for j in range(2):
        for i, w in enumerate((w_gate, w_up, w_down)):
            pltpu.make_async_copy(w.at[j], wts.at[j, i, pl.ds(0, fh)], wl_r.at[j, i]).start()
    pl.semaphore_wait(barrier, len(partners))

    nb = 16 * ((n + 2 * topk + 31) // 32)
    cuts = [pl.ds(0, nb), pl.ds(nb, n + 2 * topk - nb)]
    for u in range(2):
        mine = tok.at[E, cuts[u]]
        send(mine, mine, za_s.at[0, 0, u], za_r.at[0, 0, u], z_up)
        send(mine, mine, za_s.at[1, 0, u], za_r.at[1, 0, u], z_down)
    send(tok.at[E], tok.at[E], sb_s.at[0], sb_r.at[0], other)
    for m in range(1, SIDE):
        to = (E, y * SIDE + mod(x + m, SIDE))
        send(gains.at[T], gains.at[T], gn_s.at[0, m], gn_r.at[0, m], to)

    for i, w in enumerate((w_gate, w_up, w_down)):
        for j in range(2):
            a, b = axes(j)
            mate = mod(a + 1 - 2 * lax.rem(a + c, 2), SIDE)
            send(w.at[j], wts.at[j, i, pl.ds(fh, fh)], w_s.at[j, i], w_r.at[j, i], device(j, mate, b))

    r_iota = lax.broadcasted_iota(jnp.int32, (two, 2 * n), 0).astype(F32)
    lane = lax.broadcasted_iota(jnp.int32, (1, 2 * n), 1)
    shift = jnp.where(lane >= n, float(capacity), 0.0)
    here = (2 * E).astype(F32)

    def select(r):
        p = mod(jnp.where(r < H, z + r, z + H - 1 - r), Z)
        got(tok.at[2 * p + 1 - c], sb_s.at[r], sb_r.at[r])
        m0 = tok[2 * p, n : n + 2 * topk, :].astype(F32)
        m1 = tok[2 * p + 1, n : n + 2 * topk, :].astype(F32)

        def both(i, l):
            return jnp.concatenate(
                [
                    m0[i * topk : (i + 1) * topk, l * n : (l + 1) * n],
                    m1[i * topk : (i + 1) * topk, l * n : (l + 1) * n],
                ],
                axis=1,
            )

        idp, high, low, pos = both(0, 0), both(0, 1), both(1, 0), both(1, 1)
        picked = []
        for j in range(2):
            hit = idp == here + float(j)
            named = jnp.sum(jnp.where(hit, 1.0, 0.0), axis=0, keepdims=True)
            slot = jnp.sum(jnp.where(hit, pos, 0.0), axis=0, keepdims=True)
            wh = jnp.sum(jnp.where(hit, high, 0.0), axis=0, keepdims=True)
            wo = jnp.sum(jnp.where(hit, low, 0.0), axis=0, keepdims=True)
            slot = jnp.where(named > 0.5, slot + shift, -1.0)
            taken = jnp.where(r_iota == slot, 1.0, 0.0)
            sw[r, j * two : (j + 1) * two, :] = (taken * wh).astype(BF)
            sw[r, (2 + j) * two : (3 + j) * two, :] = (taken * wo).astype(BF)
            picked.append(taken.astype(BF))
        pair = tok[pl.ds(2 * p, 2), 0:n, :].reshape(2 * n, wide)
        taken = dot(jnp.concatenate(picked, axis=0), pair, 1, 0).astype(BF)
        rows[0, r] = taken[0:two, :]
        rows[1, r] = taken[two : 2 * two, :]

    def z_step(s, carry):
        pr, po = mod(z - 1 - s, Z), mod(z + 1 + s, Z)
        er, eo = 2 * pr + c, 2 * po + c
        for u in range(2):
            br, bo = tok.at[er, cuts[u]], tok.at[eo, cuts[u]]
            got(br, za_s.at[0, s, u], za_r.at[0, s, u])

            @pl.when(s < H - 1)
            def _():
                send(br, br, za_s.at[0, s + 1, u], za_r.at[0, s + 1, u], z_up)
                got(bo, za_s.at[1, s, u], za_r.at[1, s, u])

            @pl.when(s < H - 2)
            def _():
                send(bo, bo, za_s.at[1, s + 1, u], za_r.at[1, s + 1, u], z_down)

        send(tok.at[er], tok.at[er], sb_s.at[H + s], sb_r.at[H + s], other)

        @pl.when(s < H - 1)
        def _():
            send(tok.at[eo], tok.at[eo], sb_s.at[s + 1], sb_r.at[s + 1], other)

        select(s)

        @pl.when(s > 0)
        def _():
            select(H + s - 1)

        return carry

    def mine_of(j, ch, half):
        return rows.at[j, pl.ds(H * half + Q * ch, Q)]

    def scatter(ch):
        for j in range(2):
            a, b = axes(j)
            sh = b * SIDE + a
            pltpu.make_async_copy(
                mine_of(j, ch, lax.rem(a, 2)), gath.at[j, ch, sh], a_r.at[j, ch, 0]
            ).start()
            for k in (1, 3, 2):
                to = mod(a - k, SIDE)
                send(
                    mine_of(j, ch, lax.rem(to, 2)), gath.at[j, ch, sh],
                    a_s.at[j, ch, k], a_r.at[j, ch, k], device(j, to, b),
                )

    lax.fori_loop(0, Q + 1, z_step, 0)
    scatter(0)
    for m in range(1, SIDE):
        got(gains.at[y * SIDE + mod(x - m, SIDE)], gn_s.at[0, m], gn_r.at[0, m])
    line = gains.at[pl.ds(y * SIDE, SIDE)]
    for m in range(1, SIDE):
        to = (E, mod(y + m, SIDE) * SIDE + x)
        send(line, line, gn_s.at[1, m], gn_r.at[1, m], to)
    lax.fori_loop(Q + 1, H, z_step, 0)
    select(Z - 1)
    scatter(1)

    def forward(j, ch, k):
        a, b = axes(j)
        piece = gath.at[j, ch, b * SIDE + mod(a + k, SIDE)]
        for way, d in ((0, 1), (1, -1)):
            send(
                piece, piece, b_s.at[j, ch, k, way], b_r.at[j, ch, k, way],
                device(j, a, mod(b + d, SIDE)),
            )

    def near(ch):
        for j in range(2):
            a, b = axes(j)
            pltpu.make_async_copy(
                mine_of(j, ch, lax.rem(a, 2)), gath.at[j, ch, b * SIDE + a], a_r.at[j, ch, 0]
            ).wait()
            forward(j, ch, 0)

        def step(i, carry):
            j, k = lax.rem(i, 2), lax.div(i, 2)
            a, b = axes(j)
            sh = b * SIDE + mod(a + k, SIDE)
            got(gath.at[j, ch, sh], a_s.at[j, ch, k], a_r.at[j, ch, k])
            forward(j, ch, k)
            return carry

        lax.fori_loop(2, 2 * SIDE, step, 0)

    def multiply(j, ch, sh):
        piece = gath[j, ch, sh].reshape(chunk_rows, wide).astype(F32)
        ssq[j, ch] += piece * piece
        piece = (piece * gains[owner(j, sh), 0:1, :]).astype(BF)
        col = column(j, sh)
        accg[j, ch] += dot(piece, wts[j, 0, :, col], 1, 1)
        accu[j, ch] += dot(piece, wts[j, 1, :, col], 1, 1)

    def multiply_near(ch):
        def step(i, carry):
            j, k = lax.rem(i, 2), lax.div(i, 2)
            multiply(j, ch, axes(j)[1] * SIDE + k)
            return carry

        lax.fori_loop(0, 2 * SIDE, step, 0)

    def side(ch, work):
        def step(i, carry):
            j, k = lax.rem(i, 2), lax.div(i, 2)
            a, b = axes(j)
            low = mod(b - 1, SIDE) * SIDE + mod(a + k, SIDE)
            high = mod(b + 1, SIDE) * SIDE + mod(a + k, SIDE)
            got(gath.at[j, ch, low], b_s.at[j, ch, k, 0], b_r.at[j, ch, k, 0])

            @pl.when(lax.rem(k, 2) == 0)
            def _():
                piece = gath.at[j, ch, low]
                to = device(j, a, mod(b + 1, SIDE))
                send(piece, piece, f_s.at[j, ch, k], f_r.at[j, ch, k], to)

            got(gath.at[j, ch, high], b_s.at[j, ch, k, 1], b_r.at[j, ch, k, 1])

            @pl.when(lax.rem(k, 2) == 1)
            def _():
                piece = gath.at[j, ch, high]
                to = device(j, a, mod(b - 1, SIDE))
                send(piece, piece, f_s.at[j, ch, k], f_r.at[j, ch, k], to)

            if work:
                multiply(j, ch, low)
                multiply(j, ch, high)
            return carry

        lax.fori_loop(0, 2 * SIDE, step, 0)

    def multiply_side(ch):
        def step(i, carry):
            j, k = lax.rem(i, 2), lax.div(i, 2)
            b = axes(j)[1]
            multiply(j, ch, mod(b - 1, SIDE) * SIDE + k)
            multiply(j, ch, mod(b + 1, SIDE) * SIDE + k)
            return carry

        lax.fori_loop(0, 2 * SIDE, step, 0)

    def far(ch):
        def step(i, carry):
            j, k = lax.rem(i, 2), lax.div(i, 2)
            a, b = axes(j)
            sh = mod(b + 2, SIDE) * SIDE + mod(a + k, SIDE)
            got(gath.at[j, ch, sh], f_s.at[j, ch, k], f_r.at[j, ch, k])
            multiply(j, ch, sh)
            return carry

        lax.fori_loop(0, 2 * SIDE, step, 0)

    def activate(ch):
        for j in range(2):
            total = jnp.sum(ssq[j, ch], axis=1, keepdims=True)
            scale = lax.rsqrt(total / width + epsilon)
            g = accg[j, ch] * scale
            inner[j, ch] = (g / (1.0 + jnp.exp(-g)) * (accu[j, ch] * scale)).astype(BF)

    def cuts_of(rc):
        first = 2 * A * (rc % 2)
        return pl.ds(first, A), pl.ds(first + A, A), pl.ds(first, 2 * A)

    def ends(j):
        a, b = axes(j)
        return device(j, a, mod(b + 1, SIDE)), device(j, a, mod(b - 1, SIDE))

    def hand_out(rc, d):
        ch, (lo, hi, _) = rc // 2, cuts_of(rc)
        slot = pl.ds(A * (rc % 2), A)
        for j in range(2):
            above, below = ends(j)
            bundle = part.at[j, ch, pl.ds(mod(axes(j)[1] + d, SIDE) * SIDE, SIDE)]
            ss, rs = r1_s.at[j, rc], r1_r.at[j, rc]
            if d == 2:
                send(bundle.at[:, lo], hop.at[j, ch, 0, :, slot], ss.at[0], rs.at[0], above)
                send(bundle.at[:, hi], hop.at[j, ch, 1, :, slot], ss.at[1], rs.at[1], below)
            elif d == 1:
                send(bundle.at[:, hi], from_l.at[j, ch, :, hi], ss.at[2], rs.at[2], above)
            elif d == 3:
                send(bundle.at[:, lo], from_r.at[j, ch, :, lo], ss.at[3], rs.at[3], below)

    def down(ch, d):
        def step(i, carry):
            j, aa = lax.rem(i, 2), lax.div(i, 2)
            sh = mod(axes(j)[1] + d, SIDE) * SIDE + aa
            made = dot(inner[j, ch], wts[j, 2, :, column(j, sh)], 1, 0).astype(BF)
            part[j, ch, sh] = made.reshape(Q, two, wide)
            return carry

        lax.fori_loop(0, 2 * SIDE, step, 0)

    def hops(rc):
        ch, (lo, hi, _) = rc // 2, cuts_of(rc)
        slot = pl.ds(A * (rc % 2), A)
        for way, (d, cut, target) in enumerate(((1, lo, from_l), (3, hi, from_r))):
            for j in range(2):
                first = mod(axes(j)[1] + d, SIDE) * SIDE
                here_hop = hop.at[j, ch, way, :, slot]
                got(here_hop, r1_s.at[j, rc, way], r1_r.at[j, rc, way])
                mine_part = part.at[j, ch, pl.ds(first, SIDE), cut]
                mine_part[...] = (mine_part[...].astype(F32) + here_hop[...].astype(F32)).astype(BF)
                send(
                    mine_part, target.at[j, ch, :, cut],
                    r2_s.at[j, rc, way], r2_r.at[j, rc, way], ends(j)[way],
                )

    def columns(rc):
        ch, (lo, hi, whole) = rc // 2, cuts_of(rc)
        for j in range(2):
            a, b = axes(j)
            got(from_l.at[j, ch, :, hi], r1_s.at[j, rc, 2], r1_r.at[j, rc, 2])
            got(from_r.at[j, ch, :, lo], r1_s.at[j, rc, 3], r1_r.at[j, rc, 3])
            got(from_l.at[j, ch, :, lo], r2_s.at[j, rc, 0], r2_r.at[j, rc, 0])
            got(from_r.at[j, ch, :, hi], r2_s.at[j, rc, 1], r2_r.at[j, rc, 1])

            def step(i, carry, j=j, a=a, b=b):
                m = lax.rem(SIDE + 2 - i, SIDE)
                aa = mod(a + m, SIDE)
                mixed = (
                    part[j, ch, b * SIDE + aa, whole].astype(F32)
                    + from_l[j, ch, aa, whole].astype(F32)
                    + from_r[j, ch, aa, whole].astype(F32)
                )
                vsum[j, ch, m, whole] = mixed.astype(BF)

                @pl.when(m > 0)
                def _():
                    send(
                        vsum.at[j, ch, m, whole], cross.at[j, ch, m, whole], c_s.at[j, rc, m],
                        c_r.at[j, rc, m], device(j, aa, b),
                    )

                return carry

            lax.fori_loop(0, SIDE, step, 0)

    def finish(rc):
        ch, (_, _, whole) = rc // 2, cuts_of(rc)
        for j in range(2):
            own = lax.rem(axes(j)[0], 2)
            for m in (1, 3, 2):
                got(cross.at[j, ch, m, whole], c_s.at[j, rc, m], c_r.at[j, rc, m])
            final[j, pl.ds(H * (1 - own) + 2 * A * rc, 2 * A)] = (
                cross[j, ch, 1, whole].astype(F32) + cross[j, ch, 3, whole].astype(F32)
            ).astype(BF)
            final[j, pl.ds(H * own + 2 * A * rc, 2 * A)] = (
                vsum[j, ch, 0, whole].astype(F32) + cross[j, ch, 2, whole].astype(F32)
            ).astype(BF)

        def step(i, carry):
            combine(2 * A * (rc + 1) - 1 - lax.div(i, 2) + H * lax.rem(i + 1, 2))
            return carry

        lax.fori_loop(0, 4 * A, step, 0)

    def combine(r):
        stacked = jnp.concatenate([final[0, r], final[1, r]], axis=0)
        stacked = jnp.concatenate([stacked, stacked], axis=0)
        made = dot(sw[r], stacked, 0, 0).astype(BF)
        cont[r, 0] = made[0:n, :]
        cont[r, 1] = made[n : 2 * n, :]
        send(cont.at[r, 1 - c], sib.at[r], cs_s.at[r], cs_r.at[r], other)

    hn = n // 2

    def pass_on(way, s, r, to):
        got(sib.at[r], cs_s.at[r], cs_r.at[r])
        for u in range(2):
            cut = pl.ds(u * hn, hn)
            mixed = cont[r, c, cut].astype(F32) + sib[r, cut].astype(F32)
            if s:
                got(zin.at[way, s - 1, cut], q_s.at[way, s - 1, u], q_r.at[way, s - 1, u])
                mixed = mixed + zin[way, s - 1, cut].astype(F32)
            cont[r, c, cut] = mixed.astype(BF)
            send(
                cont.at[r, c, cut], zin.at[way, s, cut], q_s.at[way, s, u], q_r.at[way, s, u], to
            )

    def right(s):
        pass_on(0, s, Z - 1 if s == 0 else H - s, z_up)

    def leftward(s):
        pass_on(1, s, Z - 2 - s, z_down)

    def left_start():
        for m in range(1, SIDE):
            left(gains.at[0], gn_s.at[0, m], gn_r.at[0, m])
            left(line, gn_s.at[1, m], gn_r.at[1, m])

        def step(s, carry):
            for u in range(2):
                left(tok.at[0, cuts[u]], za_s.at[0, s, u], za_r.at[0, s, u])

                @pl.when(s < H - 1)
                def _():
                    left(tok.at[0, cuts[u]], za_s.at[1, s, u], za_r.at[1, s, u])

            left(tok.at[0], sb_s.at[s], sb_r.at[s])
            left(tok.at[0], sb_s.at[H + s], sb_r.at[H + s])
            return carry

        lax.fori_loop(0, H, step, 0)
        for j in range(2):
            for i, w in enumerate((w_gate, w_up, w_down)):
                left(w.at[j], w_s.at[j, i], w_r.at[j, i])

    def left_pieces():
        def step(i, carry):
            j, ch, k = lax.rem(i, 2), lax.rem(lax.div(i, 2), 2), lax.div(i, 4)
            piece = gath.at[j, ch, 0]

            @pl.when(k > 0)
            def _():
                left(piece, a_s.at[j, ch, k], a_r.at[j, ch, k])

            left(piece, b_s.at[j, ch, k, 0], b_r.at[j, ch, k, 0])
            left(piece, b_s.at[j, ch, k, 1], b_r.at[j, ch, k, 1])
            left(piece, f_s.at[j, ch, k], f_r.at[j, ch, k])
            return carry

        lax.fori_loop(0, 4 * SIDE, step, 0)

    def left_part(rc):
        for j in range(2):
            for k in range(SIDE):
                left(hop.at[0, 0, 0, :, pl.ds(0, A)], r1_s.at[j, rc, k], r1_r.at[j, rc, k])
                if k:
                    left(cross.at[0, 0, 0, pl.ds(0, 2 * A)], c_s.at[j, rc, k], c_r.at[j, rc, k])
                if k < 2:
                    left(hop.at[0, 0, 0, :, pl.ds(0, A)], r2_s.at[j, rc, k], r2_r.at[j, rc, k])

    def left_ring(s, carry):
        for u in range(2):
            cut = pl.ds(u * hn, hn)
            left(zin.at[0, 0, cut], q_s.at[0, s, u], q_r.at[0, s, u])

            @pl.when(s < H - 1)
            def _():
                left(zin.at[1, 0, cut], q_s.at[1, s, u], q_r.at[1, s, u])

        return carry

    def left_cont(r, carry):
        left(sib.at[0], cs_s.at[r], cs_r.at[r])
        return carry

    accg[...] = jnp.zeros_like(accg)
    accu[...] = jnp.zeros_like(accu)
    ssq[...] = jnp.zeros_like(ssq)
    near(1)
    for m in range(1, SIDE):
        got(gains.at[pl.ds(mod(y - m, SIDE) * SIDE, SIDE)], gn_s.at[1, m], gn_r.at[1, m])

    def weights_here(kinds):
        for i in kinds:
            for j in range(2):
                w = (w_gate, w_up, w_down)[i]
                pltpu.make_async_copy(w.at[j], wts.at[j, i, pl.ds(0, fh)], wl_r.at[j, i]).wait()
                got(wts.at[j, i, pl.ds(fh, fh)], w_s.at[j, i], w_r.at[j, i])

    near(0)
    weights_here((0, 1, 2))
    multiply_near(1)
    side(1, True)
    side(0, True)
    multiply_near(0)
    far(1)
    activate(1)
    for d in (2, 1, 3, 0):
        down(1, d)
        hand_out(3, d)
        hand_out(2, d)
    far(0)
    activate(0)
    hops(3)
    down(0, 2)
    down(0, 1)
    hops(2)
    down(0, 3)
    columns(3)
    for d in (2, 1, 3):
        hand_out(1, d)
    left_start()
    down(0, 0)
    left_pieces()
    columns(2)
    for d in (2, 1, 3):
        hand_out(0, d)
    finish(3)
    right(0)
    hops(1)
    right(1)
    leftward(0)
    finish(2)
    hops(0)
    right(2)
    columns(1)
    right(3)
    leftward(1)
    finish(1)
    columns(0)
    left_part(3)
    left_part(2)
    left_part(1)
    right(4)
    leftward(2)
    right(5)
    leftward(3)
    finish(0)
    right(6)
    leftward(4)
    right(7)
    leftward(5)
    leftward(6)
    got(sib.at[0], cs_s.at[0], cs_r.at[0])
    for u in range(2):
        cut = pl.ds(u * hn, hn)
        got(zin.at[1, H - 2, cut], q_s.at[1, H - 2, u], q_r.at[1, H - 2, u])
        got(zin.at[0, H - 1, cut], q_s.at[0, H - 1, u], q_r.at[0, H - 1, u])
        out[cut] = (
            cont[0, c, cut].astype(F32)
            + sib[0, cut].astype(F32)
            + zin[1, H - 2, cut].astype(F32)
            + zin[0, H - 1, cut].astype(F32)
        ).astype(BF)

    left_part(0)
    lax.fori_loop(0, H, left_ring, 0)
    lax.fori_loop(0, Z, left_cont, 0)


def body(hidden_in, norm_gain, expert_ids, route_weights, w_gate, w_up, w_down):
    n, wide = hidden_in.shape
    topk = expert_ids.shape[1]
    fh = w_gate.shape[1]
    groups = lax.axis_size("expert")
    Z = groups // 2
    H, Q = Z // 2, Z // 4
    capacity = min(n, 3 * n * topk // (2 * 2 * groups))
    two = 2 * capacity
    vm, dma = pltpu.VMEM, pltpu.SemaphoreType.DMA
    shards = SIDE * SIDE
    scratch = [
        vm((groups, n + 2 * topk, wide), BF),
        vm((2, Z, two, wide), BF),
        vm((2, 2, shards, Q, two, wide), BF),
        vm((2, 3, 2 * fh, shards * wide), BF),
        vm((2, 2, Q * two, 2 * fh), F32),
        vm((2, 2, Q * two, 2 * fh), F32),
        vm((2, 2, Q * two, wide), F32),
        vm((2, 2, Q * two, 2 * fh), BF),
        vm((2, 2, shards, Q, two, wide), BF),
        vm((2, 2, 2, SIDE, Q // 2, two, wide), BF),
        vm((2, 2, SIDE, Q, two, wide), BF),
        vm((2, 2, SIDE, Q, two, wide), BF),
        vm((2, 2, SIDE, Q, two, wide), BF),
        vm((2, 2, SIDE, Q, two, wide), BF),
        vm((2, Z, two, wide), BF),
        vm((Z, 4 * two, 2 * n), BF),
        vm((Z, 2, n, wide), BF),
        vm((Z, n, wide), BF),
        vm((2, H, n, wide), BF),
        vm((shards, 8, wide), F32),
        dma((2, SIDE)), dma((2, SIDE)),
        dma((2, H, 2)), dma((2, H, 2)),
        dma((Z,)), dma((Z,)),
        dma((2, 3)), dma((2, 3)), dma((2, 3)),
        dma((2, 2, SIDE)), dma((2, 2, SIDE)),
        dma((2, 2, SIDE, 2)), dma((2, 2, SIDE, 2)),
        dma((2, 2, SIDE)), dma((2, 2, SIDE)),
        dma((2, 4, SIDE)), dma((2, 4, SIDE)),
        dma((2, 4, 2)), dma((2, 4, 2)),
        dma((2, 4, SIDE)), dma((2, 4, SIDE)),
        dma((Z,)), dma((Z,)),
        dma((2, H, 2)), dma((2, H, 2)),
    ]
    vmem = pl.BlockSpec(memory_space=pltpu.VMEM)
    anywhere = pl.BlockSpec(memory_space=pl.ANY)
    return pl.pallas_call(
        functools.partial(kernel, Z, capacity, wide * shards),
        out_shape=jax.ShapeDtypeStruct((n, wide), BF),
        in_specs=[vmem, vmem, vmem, vmem, anywhere, anywhere, anywhere],
        out_specs=vmem,
        scratch_shapes=scratch,
        compiler_params=pltpu.CompilerParams(
            collective_id=0, has_side_effects=True, vmem_limit_bytes=58 * 2**20
        ),
    )(hidden_in, norm_gain[None, :], expert_ids, route_weights, w_gate, w_up, w_down)


def solution(mesh):
    placed = (
        P("expert", "tensor"),
        P("tensor"),
        P("expert", None),
        P("expert", None),
        P("expert", "tensor", None),
        P("expert", "tensor", None),
        P("expert", "tensor", None),
    )
    return jax.shard_map(
        body, mesh=mesh, in_specs=placed, out_specs=P("expert", "tensor"), check_vma=False
    )
```

```python
import functools

import jax
import jax.numpy as jnp
from jax import lax
from jax.experimental import pallas as pl
from jax.experimental.pallas import tpu as pltpu
from jax.sharding import PartitionSpec as P

epsilon = 1e-06
SIDE = 4
BF = jnp.bfloat16
F32 = jnp.float32


def dot(a, b, ca, cb):
    return lax.dot_general(a, b, (((ca,), (cb,)), ((), ())), preferred_element_type=F32)


def kernel(
    Z, capacity, width,
    hid, gain, ids_in, weights_in, w_gate, w_up, w_down, out,
    tok, rows, gath, wts, accg, accu, ssq, inner, part, hop, from_l, from_r, vsum, cross, final,
    sw, cont, sib, zin, gains,
    gn_s, gn_r, za_s, za_r, sb_s, sb_r, wl_r, w_s, w_r, a_s, a_r, b_s, b_r, f_s, f_r,
    r1_s, r1_r, r2_s, r2_r, c_s, c_r, cs_s, cs_r, q_s, q_r,
):
    H = Z // 2
    Q = H // 2
    A = Q // 4
    n, wide = hid.shape
    fh = w_gate.shape[1]
    topk = ids_in.shape[1]
    experts = 4 * Z
    two = 2 * capacity
    chunk_rows = Q * two
    mesh_ids = pl.DeviceIdType.MESH

    E = lax.axis_index("expert")
    T = lax.axis_index("tensor")
    z, c = lax.div(E, 2), lax.rem(E, 2)
    y, x = lax.div(T, SIDE), lax.rem(T, SIDE)

    def mod(v, m):
        return lax.rem(v + m, m)

    def axes(j):
        return (x + j * (y - x), y + j * (x - y))

    def device(j, a, b):
        return (E, (b + j * (a - b)) * SIDE + a + j * (b - a))

    def owner(j, sh):
        bb, aa = lax.div(sh, SIDE), lax.rem(sh, SIDE)
        return bb * SIDE + aa + j * (aa * SIDE + bb - bb * SIDE - aa)

    def column(j, sh):
        return pl.ds(pl.multiple_of(owner(j, sh) * wide, wide), wide)

    def send(src, dst, ssem, rsem, to):
        pltpu.make_async_remote_copy(
            src_ref=src, dst_ref=dst, send_sem=ssem, recv_sem=rsem,
            device_id=to, device_id_type=mesh_ids,
        ).start()

    def got(dst, ssem, rsem):
        pltpu.make_async_remote_copy(
            src_ref=dst, dst_ref=dst, send_sem=ssem, recv_sem=rsem,
            device_id=(E, T), device_id_type=mesh_ids,
        ).wait_recv()

    def left(src, ssem, rsem):
        pltpu.make_async_remote_copy(
            src_ref=src, dst_ref=src, send_sem=ssem, recv_sem=rsem,
            device_id=(E, T), device_id_type=mesh_ids,
        ).wait_send()

    other = (2 * z + 1 - c, T)
    z_up = (2 * mod(z + 1, Z) + c, T)
    z_down = (2 * mod(z - 1, Z) + c, T)

    barrier = pltpu.get_barrier_semaphore()
    partners = [other, z_up, z_down]
    for m in range(1, SIDE):
        partners.append((E, y * SIDE + mod(x + m, SIDE)))
        partners.append((E, mod(y + m, SIDE) * SIDE + x))
    for partner in partners:
        pl.semaphore_signal(barrier, inc=1, device_id=partner, device_id_type=mesh_ids)

    ids = ids_in[...].astype(F32).T
    wts_t = weights_in[...].T
    e_iota = lax.broadcasted_iota(jnp.int32, (experts, n), 0).astype(F32)
    hits = [e_iota == ids[k : k + 1, :] for k in range(topk)]
    chosen = jnp.zeros((experts, n), F32)
    for k in range(topk):
        chosen = chosen + jnp.where(hits[k], 1.0, 0.0)
    tri = (
        lax.broadcasted_iota(jnp.int32, (n, n), 0) < lax.broadcasted_iota(jnp.int32, (n, n), 1)
    ).astype(F32).astype(BF)
    before = dot(chosen.astype(BF), tri, 1, 0)
    pos = jnp.concatenate(
        [jnp.sum(jnp.where(hits[k], before, 0.0), axis=0, keepdims=True) for k in range(topk)],
        axis=0,
    )
    high = wts_t.astype(BF).astype(F32)
    meta = jnp.concatenate(
        [jnp.concatenate([ids, high], axis=1), jnp.concatenate([wts_t - high, pos], axis=1)],
        axis=0,
    )
    tok[E, n : n + 2 * topk, :] = meta.astype(BF)
    tok[E, 0:n, :] = hid[...]
    gains[T] = jnp.broadcast_to(gain[...], (8, wide))
    for j in range(2):
        for i, w in enumerate((w_gate, w_up, w_down)):
            pltpu.make_async_copy(w.at[j], wts.at[j, i, pl.ds(0, fh)], wl_r.at[j, i]).start()
    pl.semaphore_wait(barrier, len(partners))

    nb = 16 * ((n + 2 * topk + 31) // 32)
    cuts = [pl.ds(0, nb), pl.ds(nb, n + 2 * topk - nb)]
    for u in range(2):
        mine = tok.at[E, cuts[u]]
        send(mine, mine, za_s.at[0, 0, u], za_r.at[0, 0, u], z_up)
        send(mine, mine, za_s.at[1, 0, u], za_r.at[1, 0, u], z_down)
    send(tok.at[E], tok.at[E], sb_s.at[0], sb_r.at[0], other)
    for m in range(1, SIDE):
        to = (E, y * SIDE + mod(x + m, SIDE))
        send(gains.at[T], gains.at[T], gn_s.at[0, m], gn_r.at[0, m], to)

    for i, w in enumerate((w_gate, w_up, w_down)):
        for j in range(2):
            a, b = axes(j)
            mate = mod(a + 1 - 2 * lax.rem(a + c, 2), SIDE)
            send(w.at[j], wts.at[j, i, pl.ds(fh, fh)], w_s.at[j, i], w_r.at[j, i], device(j, mate, b))

    r_iota = lax.broadcasted_iota(jnp.int32, (two, 2 * n), 0).astype(F32)
    lane = lax.broadcasted_iota(jnp.int32, (1, 2 * n), 1)
    shift = jnp.where(lane >= n, float(capacity), 0.0)
    here = (2 * E).astype(F32)

    def select(r):
        p = mod(jnp.where(r < H, z + r, z + H - 1 - r), Z)
        got(tok.at[2 * p + 1 - c], sb_s.at[r], sb_r.at[r])
        m0 = tok[2 * p, n : n + 2 * topk, :].astype(F32)
        m1 = tok[2 * p + 1, n : n + 2 * topk, :].astype(F32)

        def both(i, l):
            return jnp.concatenate(
                [
                    m0[i * topk : (i + 1) * topk, l * n : (l + 1) * n],
                    m1[i * topk : (i + 1) * topk, l * n : (l + 1) * n],
                ],
                axis=1,
            )

        idp, high, low, pos = both(0, 0), both(0, 1), both(1, 0), both(1, 1)
        picked = []
        for j in range(2):
            hit = idp == here + float(j)
            named = jnp.sum(jnp.where(hit, 1.0, 0.0), axis=0, keepdims=True)
            slot = jnp.sum(jnp.where(hit, pos, 0.0), axis=0, keepdims=True)
            wh = jnp.sum(jnp.where(hit, high, 0.0), axis=0, keepdims=True)
            wo = jnp.sum(jnp.where(hit, low, 0.0), axis=0, keepdims=True)
            slot = jnp.where(named > 0.5, slot + shift, -1.0)
            taken = jnp.where(r_iota == slot, 1.0, 0.0)
            sw[r, j * two : (j + 1) * two, :] = (taken * wh).astype(BF)
            sw[r, (2 + j) * two : (3 + j) * two, :] = (taken * wo).astype(BF)
            picked.append(taken.astype(BF))
        pair = tok[pl.ds(2 * p, 2), 0:n, :].reshape(2 * n, wide)
        taken = dot(jnp.concatenate(picked, axis=0), pair, 1, 0).astype(BF)
        rows[0, r] = taken[0:two, :]
        rows[1, r] = taken[two : 2 * two, :]

    def z_step(s, carry):
        pr, po = mod(z - 1 - s, Z), mod(z + 1 + s, Z)
        er, eo = 2 * pr + c, 2 * po + c
        for u in range(2):
            br, bo = tok.at[er, cuts[u]], tok.at[eo, cuts[u]]
            got(br, za_s.at[0, s, u], za_r.at[0, s, u])

            @pl.when(s < H - 1)
            def _():
                send(br, br, za_s.at[0, s + 1, u], za_r.at[0, s + 1, u], z_up)
                got(bo, za_s.at[1, s, u], za_r.at[1, s, u])

            @pl.when(s < H - 2)
            def _():
                send(bo, bo, za_s.at[1, s + 1, u], za_r.at[1, s + 1, u], z_down)

        send(tok.at[er], tok.at[er], sb_s.at[H + s], sb_r.at[H + s], other)

        @pl.when(s < H - 1)
        def _():
            send(tok.at[eo], tok.at[eo], sb_s.at[s + 1], sb_r.at[s + 1], other)

        select(s)

        @pl.when(s > 0)
        def _():
            select(H + s - 1)

        return carry

    def mine_of(j, ch, half):
        return rows.at[j, pl.ds(H * half + Q * ch, Q)]

    def scatter(ch):
        for j in range(2):
            a, b = axes(j)
            sh = b * SIDE + a
            pltpu.make_async_copy(
                mine_of(j, ch, lax.rem(a, 2)), gath.at[j, ch, sh], a_r.at[j, ch, 0]
            ).start()
            for k in (1, 3, 2):
                to = mod(a - k, SIDE)
                send(
                    mine_of(j, ch, lax.rem(to, 2)), gath.at[j, ch, sh],
                    a_s.at[j, ch, k], a_r.at[j, ch, k], device(j, to, b),
                )

    lax.fori_loop(0, Q + 1, z_step, 0)
    scatter(0)
    for m in range(1, SIDE):
        got(gains.at[y * SIDE + mod(x - m, SIDE)], gn_s.at[0, m], gn_r.at[0, m])
    line = gains.at[pl.ds(y * SIDE, SIDE)]
    for m in range(1, SIDE):
        to = (E, mod(y + m, SIDE) * SIDE + x)
        send(line, line, gn_s.at[1, m], gn_r.at[1, m], to)
    lax.fori_loop(Q + 1, H, z_step, 0)
    select(Z - 1)
    scatter(1)

    def forward(j, ch, k):
        a, b = axes(j)
        piece = gath.at[j, ch, b * SIDE + mod(a + k, SIDE)]
        for way, d in ((0, 1), (1, -1)):
            send(
                piece, piece, b_s.at[j, ch, k, way], b_r.at[j, ch, k, way],
                device(j, a, mod(b + d, SIDE)),
            )

    def near(ch):
        for j in range(2):
            a, b = axes(j)
            pltpu.make_async_copy(
                mine_of(j, ch, lax.rem(a, 2)), gath.at[j, ch, b * SIDE + a], a_r.at[j, ch, 0]
            ).wait()
            forward(j, ch, 0)

        def step(i, carry):
            j, k = lax.rem(i, 2), lax.div(i, 2)
            a, b = axes(j)
            sh = b * SIDE + mod(a + k, SIDE)
            got(gath.at[j, ch, sh], a_s.at[j, ch, k], a_r.at[j, ch, k])
            forward(j, ch, k)
            return carry

        lax.fori_loop(2, 2 * SIDE, step, 0)

    def multiply(j, ch, sh):
        piece = gath[j, ch, sh].reshape(chunk_rows, wide).astype(F32)
        ssq[j, ch] += piece * piece
        piece = (piece * gains[owner(j, sh), 0:1, :]).astype(BF)
        col = column(j, sh)
        accg[j, ch] += dot(piece, wts[j, 0, :, col], 1, 1)
        accu[j, ch] += dot(piece, wts[j, 1, :, col], 1, 1)

    def multiply_near(ch):
        def step(i, carry):
            j, k = lax.rem(i, 2), lax.div(i, 2)
            multiply(j, ch, axes(j)[1] * SIDE + k)
            return carry

        lax.fori_loop(0, 2 * SIDE, step, 0)

    def side(ch, work):
        def step(i, carry):
            j, k = lax.rem(i, 2), lax.div(i, 2)
            a, b = axes(j)
            low = mod(b - 1, SIDE) * SIDE + mod(a + k, SIDE)
            high = mod(b + 1, SIDE) * SIDE + mod(a + k, SIDE)
            got(gath.at[j, ch, low], b_s.at[j, ch, k, 0], b_r.at[j, ch, k, 0])

            @pl.when(lax.rem(k, 2) == 0)
            def _():
                piece = gath.at[j, ch, low]
                to = device(j, a, mod(b + 1, SIDE))
                send(piece, piece, f_s.at[j, ch, k], f_r.at[j, ch, k], to)

            got(gath.at[j, ch, high], b_s.at[j, ch, k, 1], b_r.at[j, ch, k, 1])

            @pl.when(lax.rem(k, 2) == 1)
            def _():
                piece = gath.at[j, ch, high]
                to = device(j, a, mod(b - 1, SIDE))
                send(piece, piece, f_s.at[j, ch, k], f_r.at[j, ch, k], to)

            if work:
                multiply(j, ch, low)
                multiply(j, ch, high)
            return carry

        lax.fori_loop(0, 2 * SIDE, step, 0)

    def multiply_side(ch):
        def step(i, carry):
            j, k = lax.rem(i, 2), lax.div(i, 2)
            b = axes(j)[1]
            multiply(j, ch, mod(b - 1, SIDE) * SIDE + k)
            multiply(j, ch, mod(b + 1, SIDE) * SIDE + k)
            return carry

        lax.fori_loop(0, 2 * SIDE, step, 0)

    def far(ch):
        def step(i, carry):
            j, k = lax.rem(i, 2), lax.div(i, 2)
            a, b = axes(j)
            sh = mod(b + 2, SIDE) * SIDE + mod(a + k, SIDE)
            got(gath.at[j, ch, sh], f_s.at[j, ch, k], f_r.at[j, ch, k])
            multiply(j, ch, sh)
            return carry

        lax.fori_loop(0, 2 * SIDE, step, 0)

    def activate(ch):
        for j in range(2):
            total = jnp.sum(ssq[j, ch], axis=1, keepdims=True)
            scale = lax.rsqrt(total / width + epsilon)
            g = accg[j, ch] * scale
            inner[j, ch] = (g / (1.0 + jnp.exp(-g)) * (accu[j, ch] * scale)).astype(BF)

    def cuts_of(rc):
        first = 2 * A * (rc % 2)
        return pl.ds(first, A), pl.ds(first + A, A), pl.ds(first, 2 * A)

    def ends(j):
        a, b = axes(j)
        return device(j, a, mod(b + 1, SIDE)), device(j, a, mod(b - 1, SIDE))

    def hand_out(rc, d):
        ch, (lo, hi, _) = rc // 2, cuts_of(rc)
        slot = pl.ds(A * (rc % 2), A)
        for j in range(2):
            above, below = ends(j)
            bundle = part.at[j, ch, pl.ds(mod(axes(j)[1] + d, SIDE) * SIDE, SIDE)]
            ss, rs = r1_s.at[j, rc], r1_r.at[j, rc]
            if d == 2:
                send(bundle.at[:, lo], hop.at[j, ch, 0, :, slot], ss.at[0], rs.at[0], above)
                send(bundle.at[:, hi], hop.at[j, ch, 1, :, slot], ss.at[1], rs.at[1], below)
            elif d == 1:
                send(bundle.at[:, hi], from_l.at[j, ch, :, hi], ss.at[2], rs.at[2], above)
            elif d == 3:
                send(bundle.at[:, lo], from_r.at[j, ch, :, lo], ss.at[3], rs.at[3], below)

    def down(ch, d):
        def step(i, carry):
            j, aa = lax.rem(i, 2), lax.div(i, 2)
            sh = mod(axes(j)[1] + d, SIDE) * SIDE + aa
            made = dot(inner[j, ch], wts[j, 2, :, column(j, sh)], 1, 0).astype(BF)
            part[j, ch, sh] = made.reshape(Q, two, wide)
            return carry

        lax.fori_loop(0, 2 * SIDE, step, 0)

    def hops(rc):
        ch, (lo, hi, _) = rc // 2, cuts_of(rc)
        slot = pl.ds(A * (rc % 2), A)
        for way, (d, cut, target) in enumerate(((1, lo, from_l), (3, hi, from_r))):
            for j in range(2):
                first = mod(axes(j)[1] + d, SIDE) * SIDE
                here_hop = hop.at[j, ch, way, :, slot]
                got(here_hop, r1_s.at[j, rc, way], r1_r.at[j, rc, way])
                mine_part = part.at[j, ch, pl.ds(first, SIDE), cut]
                mine_part[...] = (mine_part[...].astype(F32) + here_hop[...].astype(F32)).astype(BF)
                send(
                    mine_part, target.at[j, ch, :, cut],
                    r2_s.at[j, rc, way], r2_r.at[j, rc, way], ends(j)[way],
                )

    def columns(rc):
        ch, (lo, hi, whole) = rc // 2, cuts_of(rc)
        for j in range(2):
            a, b = axes(j)
            got(from_l.at[j, ch, :, hi], r1_s.at[j, rc, 2], r1_r.at[j, rc, 2])
            got(from_r.at[j, ch, :, lo], r1_s.at[j, rc, 3], r1_r.at[j, rc, 3])
            got(from_l.at[j, ch, :, lo], r2_s.at[j, rc, 0], r2_r.at[j, rc, 0])
            got(from_r.at[j, ch, :, hi], r2_s.at[j, rc, 1], r2_r.at[j, rc, 1])

            def step(i, carry, j=j, a=a, b=b):
                m = lax.rem(SIDE + 2 - i, SIDE)
                aa = mod(a + m, SIDE)
                mixed = (
                    part[j, ch, b * SIDE + aa, whole].astype(F32)
                    + from_l[j, ch, aa, whole].astype(F32)
                    + from_r[j, ch, aa, whole].astype(F32)
                )
                vsum[j, ch, m, whole] = mixed.astype(BF)

                @pl.when(m > 0)
                def _():
                    send(
                        vsum.at[j, ch, m, whole], cross.at[j, ch, m, whole], c_s.at[j, rc, m],
                        c_r.at[j, rc, m], device(j, aa, b),
                    )

                return carry

            lax.fori_loop(0, SIDE, step, 0)

    def finish(rc):
        ch, (_, _, whole) = rc // 2, cuts_of(rc)
        for j in range(2):
            own = lax.rem(axes(j)[0], 2)
            for m in (1, 3, 2):
                got(cross.at[j, ch, m, whole], c_s.at[j, rc, m], c_r.at[j, rc, m])
            final[j, pl.ds(H * (1 - own) + 2 * A * rc, 2 * A)] = (
                cross[j, ch, 1, whole].astype(F32) + cross[j, ch, 3, whole].astype(F32)
            ).astype(BF)
            final[j, pl.ds(H * own + 2 * A * rc, 2 * A)] = (
                vsum[j, ch, 0, whole].astype(F32) + cross[j, ch, 2, whole].astype(F32)
            ).astype(BF)

        def step(i, carry):
            combine(2 * A * (rc + 1) - 1 - lax.div(i, 2) + H * lax.rem(i + 1, 2))
            return carry

        lax.fori_loop(0, 4 * A, step, 0)

    def combine(r):
        stacked = jnp.concatenate([final[0, r], final[1, r]], axis=0)
        stacked = jnp.concatenate([stacked, stacked], axis=0)
        made = dot(sw[r], stacked, 0, 0).astype(BF)
        cont[r, 0] = made[0:n, :]
        cont[r, 1] = made[n : 2 * n, :]
        send(cont.at[r, 1 - c], sib.at[r], cs_s.at[r], cs_r.at[r], other)

    hn = n // 2

    def pass_on(way, s, r, to):
        got(sib.at[r], cs_s.at[r], cs_r.at[r])
        for u in range(2):
            cut = pl.ds(u * hn, hn)
            mixed = cont[r, c, cut].astype(F32) + sib[r, cut].astype(F32)
            if s:
                got(zin.at[way, s - 1, cut], q_s.at[way, s - 1, u], q_r.at[way, s - 1, u])
                mixed = mixed + zin[way, s - 1, cut].astype(F32)
            cont[r, c, cut] = mixed.astype(BF)
            send(
                cont.at[r, c, cut], zin.at[way, s, cut], q_s.at[way, s, u], q_r.at[way, s, u], to
            )

    def right(s):
        pass_on(0, s, Z - 1 if s == 0 else H - s, z_up)

    def leftward(s):
        pass_on(1, s, Z - 2 - s, z_down)

    def left_start():
        for m in range(1, SIDE):
            left(gains.at[0], gn_s.at[0, m], gn_r.at[0, m])
            left(line, gn_s.at[1, m], gn_r.at[1, m])

        def step(s, carry):
            for u in range(2):
                left(tok.at[0, cuts[u]], za_s.at[0, s, u], za_r.at[0, s, u])

                @pl.when(s < H - 1)
                def _():
                    left(tok.at[0, cuts[u]], za_s.at[1, s, u], za_r.at[1, s, u])

            left(tok.at[0], sb_s.at[s], sb_r.at[s])
            left(tok.at[0], sb_s.at[H + s], sb_r.at[H + s])
            return carry

        lax.fori_loop(0, H, step, 0)
        for j in range(2):
            for i, w in enumerate((w_gate, w_up, w_down)):
                left(w.at[j], w_s.at[j, i], w_r.at[j, i])

    def left_pieces():
        def step(i, carry):
            j, ch, k = lax.rem(i, 2), lax.rem(lax.div(i, 2), 2), lax.div(i, 4)
            piece = gath.at[j, ch, 0]

            @pl.when(k > 0)
            def _():
                left(piece, a_s.at[j, ch, k], a_r.at[j, ch, k])

            left(piece, b_s.at[j, ch, k, 0], b_r.at[j, ch, k, 0])
            left(piece, b_s.at[j, ch, k, 1], b_r.at[j, ch, k, 1])
            left(piece, f_s.at[j, ch, k], f_r.at[j, ch, k])
            return carry

        lax.fori_loop(0, 4 * SIDE, step, 0)

    def left_part(rc):
        for j in range(2):
            for k in range(SIDE):
                left(hop.at[0, 0, 0, :, pl.ds(0, A)], r1_s.at[j, rc, k], r1_r.at[j, rc, k])
                if k:
                    left(cross.at[0, 0, 0, pl.ds(0, 2 * A)], c_s.at[j, rc, k], c_r.at[j, rc, k])
                if k < 2:
                    left(hop.at[0, 0, 0, :, pl.ds(0, A)], r2_s.at[j, rc, k], r2_r.at[j, rc, k])

    def left_ring(s, carry):
        for u in range(2):
            cut = pl.ds(u * hn, hn)
            left(zin.at[0, 0, cut], q_s.at[0, s, u], q_r.at[0, s, u])

            @pl.when(s < H - 1)
            def _():
                left(zin.at[1, 0, cut], q_s.at[1, s, u], q_r.at[1, s, u])

        return carry

    def left_cont(r, carry):
        left(sib.at[0], cs_s.at[r], cs_r.at[r])
        return carry

    accg[...] = jnp.zeros_like(accg)
    accu[...] = jnp.zeros_like(accu)
    ssq[...] = jnp.zeros_like(ssq)
    near(1)
    for m in range(1, SIDE):
        got(gains.at[pl.ds(mod(y - m, SIDE) * SIDE, SIDE)], gn_s.at[1, m], gn_r.at[1, m])

    def weights_here(kinds):
        for i in kinds:
            for j in range(2):
                w = (w_gate, w_up, w_down)[i]
                pltpu.make_async_copy(w.at[j], wts.at[j, i, pl.ds(0, fh)], wl_r.at[j, i]).wait()
                got(wts.at[j, i, pl.ds(fh, fh)], w_s.at[j, i], w_r.at[j, i])

    near(0)
    weights_here((0, 1, 2))
    multiply_near(1)
    side(1, True)
    side(0, True)
    multiply_near(0)
    far(1)
    activate(1)
    for d in (2, 1, 3, 0):
        down(1, d)
        hand_out(3, d)
        hand_out(2, d)
    far(0)
    activate(0)
    hops(3)
    down(0, 2)
    down(0, 1)
    hops(2)
    down(0, 3)
    columns(3)
    for d in (2, 1, 3):
        hand_out(1, d)
    columns(2)
    for d in (2, 1, 3):
        hand_out(0, d)
    finish(3)
    right(0)
    down(0, 0)
    hops(1)
    left_start()
    right(1)
    leftward(0)
    left_pieces()
    finish(2)
    hops(0)
    right(2)
    columns(1)
    right(3)
    leftward(1)
    finish(1)
    columns(0)
    left_part(3)
    left_part(2)
    left_part(1)
    right(4)
    leftward(2)
    right(5)
    leftward(3)
    finish(0)
    right(6)
    leftward(4)
    right(7)
    leftward(5)
    leftward(6)
    got(sib.at[0], cs_s.at[0], cs_r.at[0])
    for u in range(2):
        cut = pl.ds(u * hn, hn)
        got(zin.at[1, H - 2, cut], q_s.at[1, H - 2, u], q_r.at[1, H - 2, u])
        got(zin.at[0, H - 1, cut], q_s.at[0, H - 1, u], q_r.at[0, H - 1, u])
        out[cut] = (
            cont[0, c, cut].astype(F32)
            + sib[0, cut].astype(F32)
            + zin[1, H - 2, cut].astype(F32)
            + zin[0, H - 1, cut].astype(F32)
        ).astype(BF)

    left_part(0)
    lax.fori_loop(0, H, left_ring, 0)
    lax.fori_loop(0, Z, left_cont, 0)


def body(hidden_in, norm_gain, expert_ids, route_weights, w_gate, w_up, w_down):
    n, wide = hidden_in.shape
    topk = expert_ids.shape[1]
    fh = w_gate.shape[1]
    groups = lax.axis_size("expert")
    Z = groups // 2
    H, Q = Z // 2, Z // 4
    capacity = min(n, 3 * n * topk // (2 * 2 * groups))
    two = 2 * capacity
    vm, dma = pltpu.VMEM, pltpu.SemaphoreType.DMA
    shards = SIDE * SIDE
    scratch = [
        vm((groups, n + 2 * topk, wide), BF),
        vm((2, Z, two, wide), BF),
        vm((2, 2, shards, Q, two, wide), BF),
        vm((2, 3, 2 * fh, shards * wide), BF),
        vm((2, 2, Q * two, 2 * fh), F32),
        vm((2, 2, Q * two, 2 * fh), F32),
        vm((2, 2, Q * two, wide), F32),
        vm((2, 2, Q * two, 2 * fh), BF),
        vm((2, 2, shards, Q, two, wide), BF),
        vm((2, 2, 2, SIDE, Q // 2, two, wide), BF),
        vm((2, 2, SIDE, Q, two, wide), BF),
        vm((2, 2, SIDE, Q, two, wide), BF),
        vm((2, 2, SIDE, Q, two, wide), BF),
        vm((2, 2, SIDE, Q, two, wide), BF),
        vm((2, Z, two, wide), BF),
        vm((Z, 4 * two, 2 * n), BF),
        vm((Z, 2, n, wide), BF),
        vm((Z, n, wide), BF),
        vm((2, H, n, wide), BF),
        vm((shards, 8, wide), F32),
        dma((2, SIDE)), dma((2, SIDE)),
        dma((2, H, 2)), dma((2, H, 2)),
        dma((Z,)), dma((Z,)),
        dma((2, 3)), dma((2, 3)), dma((2, 3)),
        dma((2, 2, SIDE)), dma((2, 2, SIDE)),
        dma((2, 2, SIDE, 2)), dma((2, 2, SIDE, 2)),
        dma((2, 2, SIDE)), dma((2, 2, SIDE)),
        dma((2, 4, SIDE)), dma((2, 4, SIDE)),
        dma((2, 4, 2)), dma((2, 4, 2)),
        dma((2, 4, SIDE)), dma((2, 4, SIDE)),
        dma((Z,)), dma((Z,)),
        dma((2, H, 2)), dma((2, H, 2)),
    ]
    vmem = pl.BlockSpec(memory_space=pltpu.VMEM)
    anywhere = pl.BlockSpec(memory_space=pl.ANY)
    return pl.pallas_call(
        functools.partial(kernel, Z, capacity, wide * shards),
        out_shape=jax.ShapeDtypeStruct((n, wide), BF),
        in_specs=[vmem, vmem, vmem, vmem, anywhere, anywhere, anywhere],
        out_specs=vmem,
        scratch_shapes=scratch,
        compiler_params=pltpu.CompilerParams(
            collective_id=0, has_side_effects=True, vmem_limit_bytes=58 * 2**20
        ),
    )(hidden_in, norm_gain[None, :], expert_ids, route_weights, w_gate, w_up, w_down)


def solution(mesh):
    placed = (
        P("expert", "tensor"),
        P("tensor"),
        P("expert", None),
        P("expert", None),
        P("expert", "tensor", None),
        P("expert", "tensor", None),
        P("expert", "tensor", None),
    )
    return jax.shard_map(
        body, mesh=mesh, in_specs=placed, out_specs=P("expert", "tensor"), check_vma=False
    )
```
